32 devices in a mesh: base: 8 (over z, x), tm: 4 (over y, core).
Axes of the slice: x: 2, y: 2, z: 4, core: 2. Of those that a mesh axis runs over, the one named last changes fastest.
Arguments:
- visibilities: bfloat16 [4, 1024, 2, 256], P('tm', 'base'), may hold values from -6 to 6
- coords: float32 [4, 1024, 2, 256], P('tm', 'base'), may hold values from -16 to 16
- counts: int32 [4, 1024], P('tm', 'base'), may hold values from 1 to 256, 157286 in all within a row
- stations: int32 [1024, 2], P('base'), may hold values from 0 to 31
- owners: int32 [1024, 1], replicated, may hold values from 0 to 7; in each aligned block of 128 rows (0 to 127, 128 to 255, ...) at most 24 rows name the same one
- offsets: int32 [1024, 2], replicated, may hold values from 0 to 224
- screens: bfloat16 [32, 2, 1024], P('base'), may hold values from -4 to 4
Outputs:
- grid_tiles: float32 [8, 256, 2, 256], P('base', 'tm')
The draws below stay inside these ranges and needn't reach their ends.
Inputs may be any that keep to these rules, and one draw needn't show every extreme that they name: `counts`: in each time block some subgrid uses all 256 slots. `owners`: among the 128 subgrids of one index of base no tile is named more than 24 times, a bound that some block reaches.
All inputs are finite; a program needn't handle non-finite values.
Results may differ from the reference program's by a relative error of at most 0.023.
Values may be sent and summed in bfloat16 or wider, within the bound.
No kernel may reach another device: no remote copies, remote signals or barrier semaphores. Data moves between devices by JAX's collectives and lax.ppermute only.
A program may use at most 64 MiB of HBM per device.

```python
import math
import jax
import jax.numpy as jnp
import numpy as np
from jax import lax

SUB = 32
PIX = 1024
S_DEV = 128
NV = 256
TILE = 256
STATIONS = 32
SUBGRIDS = 1024
TBLOCKS = 4
TILES = 8
CAP = 24


def with_ends(drawn, key, least, largest):
    index_at = [jax.random.randint(jax.random.fold_in(key, axis), (), 0, length) for axis, length in enumerate(drawn.shape)]
    main_axis = drawn.shape.index(max(drawn.shape))
    neighbour = index_at[:main_axis] + [(index_at[main_axis] + 1) % drawn.shape[main_axis]] + index_at[main_axis + 1:]
    return drawn.at[tuple(index_at)].set(least).at[tuple(neighbour)].set(largest)


def levels(rng, dims, pieces, least, high):
    gain, own = 1.0, jax.random.fold_in(rng, 6)
    for dim, blocks in pieces:
        steps = jnp.exp(jax.random.uniform(jax.random.fold_in(own, dim), (blocks,), jnp.float32, least / len(pieces), high / len(pieces)))
        gain = gain * jnp.repeat(steps, dims[dim] // blocks).reshape([-1 if axis == dim else 1 for axis in range(len(dims))])
    return gain


def profile(amount, total, reach, skew):
    loads = [(1 << 20) // math.isqrt(standing ** skew) + 1 for standing in range(2, amount + 1)]
    surplus, given = total - reach - (amount - 1), [1] * (amount - 1)
    while surplus > 0:
        free = [i for i in range(amount - 1) if given[i] < reach]
        whole, left = sum([loads[i] for i in free]), surplus
        for i in free:
            more = min(reach - given[i], max(1, left * loads[i] // whole), surplus)
            given[i] = given[i] + more
            surplus = surplus - more
    return np.array([reach] + given)


def ragged(stream_key, number_of, total, limit, skew):
    if number_of == 2:
        one = jax.random.randint(stream_key, (), max(1, total - limit), min(limit, total - 1) + 1)
        return jnp.stack([one, total - one])
    lengths = jnp.asarray(profile(number_of, total, limit, skew), jnp.int32)
    twos = (number_of - 1) // 2
    source_of, sink = lengths[1:1 + 2 * twos:2], lengths[2:2 + 2 * twos:2]
    slack = jnp.minimum(source_of - 1, limit - sink)
    passed = jax.random.randint(jax.random.fold_in(stream_key, 1), (twos,), 0, 1 << 20) % (slack + 1)
    lengths = lengths.at[1:1 + 2 * twos:2].set(source_of - passed).at[2:2 + 2 * twos:2].set(sink + passed)
    return lengths[jax.random.permutation(jax.random.fold_in(stream_key, 2), number_of)]


def deal_out(own_key, own, number, rows, amount, top, limit, slope):
    order = jax.random.permutation(own_key, amount)
    crowded, usual = load_shares(amount, rows * top, limit, slope, True), load_shares(amount, rows * top, limit, slope, False)
    places = jnp.arange(amount)

    def named(lengths, rotation):
        used = int((lengths > 0).sum())
        fixed = max(1, used // 4)
        moved = fixed + (places - fixed + rotation * (used - fixed)) % max(1, amount - fixed)
        return jnp.zeros((amount,), jnp.int32).at[order[jnp.where(places < fixed, places, moved)]].set(jnp.asarray(lengths, jnp.int32))

    lengths = jnp.where(number % 4 == 0, named(crowded, number // 4), named(usual, number - number // 4 - 1))
    mixed = jax.random.permutation(jax.random.fold_in(own, 3), amount)
    source_of, taker = mixed[0:amount // 2 * 2:2], mixed[1:amount // 2 * 2:2]
    margin = jnp.minimum(lengths[source_of] - 1, limit - lengths[taker]) // 2
    margin = jnp.where((source_of == order[0]) | (taker == order[0]) | (lengths[taker] == 0), 0, jnp.maximum(margin, 0))
    moved = jax.random.randint(jax.random.fold_in(own, 4), (amount // 2,), 0, 1 << 20) % (margin + 1)
    lengths = lengths.at[source_of].add(-moved).at[taker].add(moved)
    items = jnp.searchsorted(jnp.cumsum(lengths), jnp.arange(rows * top), side="right").astype(jnp.int32)
    listing = items.reshape(top, rows).T
    listing = listing[jax.random.permutation(jax.random.fold_in(own, 1), rows)]
    rotation = jax.random.randint(jax.random.fold_in(own, 2), (rows, 1), 0, top)
    return jnp.take_along_axis(listing, (jnp.arange(top)[None, :] + rotation) % top, axis=1)


def load_shares(number_of, total, bound, skew, full):
    loads = [(1 << 20) // math.isqrt(grade ** skew) + 1 for grade in range(1, number_of + 1)]
    largest = bound if full else min(bound, max(-(-total // number_of), total * loads[0] // sum(loads)))
    least = 1 if total - largest >= number_of - 1 else 0
    holding, surplus = [largest] + [least] * (number_of - 1), total - largest - least * (number_of - 1)
    while surplus > 0:
        candidates = [i for i in range(1, number_of) if holding[i] < largest] or [i for i in range(1, number_of) if holding[i] < bound]
        pool, remaining = sum([loads[i] for i in candidates]), surplus
        for i in candidates:
            more = min(bound - holding[i], max(1, remaining * loads[i] // pool), surplus)
            holding[i] = holding[i] + more
            surplus = surplus - more
    return np.array(holding)


def gaussian(rng, extent, spread, bound, shards=(), held_as=jnp.bfloat16):
    level = levels(rng, extent, shards, -0.22, 0.18) if shards else 1.0
    values = jax.random.normal(rng, extent, jnp.float32) * spread * level
    return jnp.minimum(jnp.maximum(values, -bound), bound).astype(held_as)


def setup_inputs(seed: int = 0) -> dict:
    splits = jax.random.split(jax.random.key(seed), 8)
    visibilities = gaussian(splits[0], (TBLOCKS, SUBGRIDS, 2, NV), 1.0, 6.0, ((0, 4), (1, 8)))
    coords = jnp.clip(jax.random.uniform(splits[1], (TBLOCKS, SUBGRIDS, 2, NV), jnp.float32, -16.0, 16.0) * levels(splits[1], (TBLOCKS, SUBGRIDS, 2, NV), ((0, 4), (1, 8)), -0.4, 0.0), -16.0, 16.0)
    counts = jax.vmap(lambda own: ragged(own, SUBGRIDS, SUBGRIDS * NV * 3 // 5, NV, 1))(jax.random.split(splits[2], TBLOCKS)).reshape((TBLOCKS, SUBGRIDS)).astype(jnp.int32)
    stations = with_ends(jax.random.randint(splits[3], (SUBGRIDS, 2), 0, STATIONS), jax.random.fold_in(splits[3], 1), 0, STATIONS - 1).astype(jnp.int32)
    owners_keys = jax.random.split(jax.random.fold_in(splits[4], 1), SUBGRIDS // S_DEV)
    owners_turns = jax.random.permutation(jax.random.fold_in(splits[4], 3), SUBGRIDS // S_DEV)
    owners = jax.vmap(lambda own, number: deal_out(jax.random.fold_in(splits[4], 2), own, number, S_DEV, TILES, 1, CAP, 2))(owners_keys, owners_turns).reshape((SUBGRIDS, 1))
    offsets = with_ends(jax.random.randint(splits[5], (SUBGRIDS, 2), 0, TILE - SUB + 1), jax.random.fold_in(splits[5], 1), 0, TILE - SUB).astype(jnp.int32)
    screens = gaussian(splits[6], (STATIONS, 2, PIX), 0.7, 4.0, ((0, 8),))
    return dict(visibilities=visibilities, coords=coords, counts=counts, stations=stations, owners=owners, offsets=offsets, screens=screens)


def taper_line(side):
    points = jnp.arange(side, dtype=jnp.float32)
    scaled = (points + 0.5 - side / 2.0) / (side / 2.0)
    return 1.0 - scaled * scaled

def fourier_tables(side):
    index_ids = jnp.arange(side, dtype=jnp.int32)
    turn_ids = index_ids[:, None] * index_ids[None, :] % side
    angles = turn_ids.astype(jnp.float32) * (2.0 * math.pi / side)
    return (jnp.cos(angles), jnp.sin(angles))

def transform(real_part, imag_part, left_cos, left_sin, right_cos, right_sin):
    highest = lax.Precision.HIGHEST
    mid_real = jnp.einsum('sml,jl->smj', real_part, right_cos, precision=highest) + jnp.einsum('sml,jl->smj', imag_part, right_sin, precision=highest)
    mid_imag = jnp.einsum('sml,jl->smj', imag_part, right_cos, precision=highest) - jnp.einsum('sml,jl->smj', real_part, right_sin, precision=highest)
    out_real = jnp.einsum('km,smj->skj', left_cos, mid_real, precision=highest) + jnp.einsum('km,smj->skj', left_sin, mid_imag, precision=highest)
    out_imag = jnp.einsum('km,smj->skj', left_cos, mid_imag, precision=highest) - jnp.einsum('km,smj->skj', left_sin, mid_real, precision=highest)
    return (out_real, out_imag)

def block_images(visibilities, coords, counts):
    slot_count = visibilities.shape[-1]
    positions = jnp.arange(SUB, dtype=jnp.float32) - SUB / 2.0
    phase_step = 2.0 * math.pi / SUB
    angle_u = coords[..., 0, None, :] * positions[:, None] * phase_step
    table_u = jnp.concatenate([jnp.cos(angle_u), jnp.sin(angle_u)], axis=-2).astype(jnp.bfloat16)
    in_count = (jnp.arange(slot_count, dtype=jnp.int32) < counts[..., None]).astype(jnp.float32)
    weight_real = visibilities[..., 0, :].astype(jnp.float32) * in_count
    weight_imag = visibilities[..., 1, :].astype(jnp.float32) * in_count
    angle_v = coords[..., 1, None, :] * positions[:, None] * phase_step
    cosine_v = jnp.cos(angle_v)
    sine_v = jnp.sin(angle_v)
    wave_real = weight_real[..., None, :] * cosine_v - weight_imag[..., None, :] * sine_v
    wave_imag = weight_real[..., None, :] * sine_v + weight_imag[..., None, :] * cosine_v
    table_v = jnp.concatenate([wave_real, wave_imag], axis=-2).astype(jnp.bfloat16)
    products = jnp.einsum('...mv,...lv->...ml', table_v.astype(jnp.float32), table_u.astype(jnp.float32))
    real_part = products[..., :SUB, :SUB] - products[..., SUB:, SUB:]
    imag_part = products[..., :SUB, SUB:] + products[..., SUB:, :SUB]
    norm_factor = 1.0 / math.sqrt(slot_count)
    return (jnp.stack([real_part, imag_part], axis=-3) * norm_factor).astype(jnp.bfloat16)

def reference(visibilities, coords, counts, stations, owners, offsets, screens):
    subgrid_total = visibilities.shape[1]
    per_map = math.gcd(subgrid_total, 64)
    map_turns = subgrid_total // per_map

    def one_group(group_id):
        first_row = group_id * per_map
        vis_part = lax.dynamic_slice_in_dim(visibilities, first_row, per_map, 1)
        coord_part = lax.dynamic_slice_in_dim(coords, first_row, per_map, 1)
        count_part = lax.dynamic_slice_in_dim(counts, first_row, per_map, 1)
        pair_part = lax.dynamic_slice_in_dim(stations, first_row, per_map, 0)
        partial_value = block_images(vis_part, coord_part, count_part)
        summed = lax.optimization_barrier(jnp.sum(partial_value.astype(jnp.float32), axis=0))
        first_side = screens[pair_part[:, 0]].astype(jnp.float32).reshape(per_map, 2, SUB, SUB)
        second_side = screens[pair_part[:, 1]].astype(jnp.float32).reshape(per_map, 2, SUB, SUB)
        gain_real = first_side[:, 0] * second_side[:, 0] + first_side[:, 1] * second_side[:, 1]
        gain_imag = first_side[:, 0] * second_side[:, 1] - first_side[:, 1] * second_side[:, 0]
        taper_row = taper_line(SUB)
        window = taper_row[:, None] * taper_row[None, :]
        x_real = (summed[:, 0] * gain_real - summed[:, 1] * gain_imag) * window
        x_imag = (summed[:, 0] * gain_imag + summed[:, 1] * gain_real) * window
        cos_table, sin_table = fourier_tables(SUB)
        out_real, out_imag = transform(x_real, x_imag, cos_table, sin_table, cos_table, sin_table)
        return (jnp.stack([out_real, out_imag], axis=1) / SUB).astype(jnp.bfloat16)
    subgrids = lax.map(one_group, jnp.arange(map_turns, dtype=jnp.int32))
    subgrids = subgrids.reshape(subgrid_total, 2, SUB, SUB)
    cell_ids = jnp.arange(SUB, dtype=jnp.int32)
    row_ids = offsets[:, 0, None] + cell_ids[None, :]
    col_ids = offsets[:, 1, None] + cell_ids[None, :]
    part_ids = jnp.arange(2, dtype=jnp.int32)
    grid_tiles = jnp.zeros((TILES, TILE, 2, TILE), jnp.float32)
    grid_tiles = grid_tiles.at[owners[:, 0, None, None, None], row_ids[:, None, :, None], part_ids[None, :, None, None], col_ids[:, None, None, :]].add(subgrids.astype(jnp.float32))
    return grid_tiles
```

```python
import functools
import math

import jax
import jax.numpy as jnp
import numpy as np
from jax import lax
from jax.experimental import pallas as pl
from jax.experimental.pallas import tpu as pltpu
from jax.sharding import PartitionSpec as P

SUB = 32
TILE = 256
LANES = 128
SINE = (4.442883014678955, -7.308245658874512, 3.6063544750213623, -0.8461129069328308, 0.10982698202133179)
COSINE = (1.4142135381698608, -6.978850841522217, 5.7394609451293945, -1.8835626224777222, 0.31069815158843994)
PARAMS = dict(compiler_params=pltpu.CompilerParams(vmem_limit_bytes=48 * 1024 * 1024))


def iota(shape, axis):
    return lax.broadcasted_iota(jnp.int32, shape, axis)


def turn(x):
    t = x - jnp.round(x)
    u = t * t
    s = ((((SINE[4] * u + SINE[3]) * u + SINE[2]) * u + SINE[1]) * u + SINE[0]) * t
    c = (((COSINE[4] * u + COSINE[3]) * u + COSINE[2]) * u + COSINE[1]) * u + COSINE[0]
    return 1.0 - s * s, s * c


def times(xr, xi, yr, yi):
    return xr * yr - xi * yi, xr * yi + xi * yr


def bit_reverse(i, size):
    out = 0
    while size > 1:
        out, i, size = out * 2 + i % 2, i // 2, size // 2
    return out


def column_of(lane):
    half = SUB // 2
    return jnp.where(lane < half, lane + half, SUB - 1 - lane)


def images_kernel(T, L, counts, offsets, coords, vis, keep, send, z1r, z1i, z2r, z2i, vs, cs):
    Q, Q2 = SUB // T, SUB // T // 2
    a, base = lax.axis_index("tm"), lax.axis_index("base")
    first = base * L
    step1, step2 = T // 4, T // 2
    sign1 = 1 - 2 * ((a // step1) % 2)
    sign2 = 1 - 2 * ((a // step2) % 2)
    sign1f, flip = sign1.astype(jnp.float32), (sign1 * sign2).astype(jnp.float32)

    R = 16
    rho, lane = iota((R, LANES), 0), iota((R, LANES), 1)
    owner, block, part = rho // 4, (rho // 2) % 2, rho % 2
    slot = lane + LANES * block
    rate1 = jnp.where(part == 0, 8.0 / SUB, sign1f * (step1 / SUB))
    flips = jnp.where(part == 0, 1.0, flip)
    crossed = jnp.where(part == 0, -1.0, 1.0)

    def pick(values):
        out = values[-1]
        for k in range(len(values) - 2, -1, -1):
            out = jnp.where(owner == k, values[k], out)
        return out

    def prepare(i, carry):
        rows = pl.ds(pl.multiple_of(i * R, R), R)
        subs = [i * 4 + k for k in range(4)]
        row_off = [offsets[0, first + s] for s in subs]
        col_off = [offsets[1, first + s] for s in subs]
        odd = [(r + c) % 2 for r, c in zip(row_off, col_off)]
        signs = [(1 - 2 * o).astype(jnp.float32) for o in odd]
        moved = jnp.where(
            part == 0,
            pick([(c % SUB).astype(jnp.float32) for c in col_off]),
            pick([(r % SUB).astype(jnp.float32) for r in row_off]),
        )
        c = coords[rows, :] + moved
        cs[rows, :] = c
        r1, i1 = turn(c * rate1)
        z1r[rows, :] = r1
        z1i[rows, :] = i1
        z2r[rows, :] = r1 * r1 - i1 * i1
        z2i[rows, :] = 2.0 * r1 * i1 * flips
        along = jnp.where(part == 0, c, pltpu.roll(c, 1, 0))
        hr, hi = turn(along * (-0.5 / SUB))
        x = vis[rows, :].astype(jnp.float32)
        x = jnp.where(slot < pick([counts[0, s] for s in subs]), x * pick(signs), 0.0)
        other = jnp.where(part == 0, pltpu.roll(x, R - 1, 0), pltpu.roll(x, 1, 0))
        vs[rows, :] = x * hr + other * (hi * crossed)
        return carry

    lax.fori_loop(0, 4 * L // R, prepare, 0, unroll=2)

    rho8 = iota((8, LANES), 0)
    rate_u = (rho8.astype(jnp.float32) + 0.5) * (1.0 / SUB)
    delta, q = rho8 // Q, rho8 % Q
    group = max(1, 8 // Q)
    rate_v = (T * q + (a ^ delta) - SUB // 2).astype(jnp.float32) * (1.0 / SUB)
    low = iota((8, LANES), 1) < LANES // 2

    def row(ref, r):
        return jnp.broadcast_to(ref[pl.ds(r, 1), :], (8, LANES))

    def one(s, carry):
        lhs_r, lhs_i, cos_u, sin_u = [], [], [], []
        for b in range(2):
            ru = s * 4 + b * 2
            rv = ru + 1
            c0, s0 = turn(row(cs, ru) * rate_u)
            c1, s1 = times(c0, s0, row(z1r, ru), row(z1i, ru))
            cos_u.append(jnp.concatenate([c0, c1], 0).astype(jnp.bfloat16))
            sin_u.append(jnp.concatenate([s0, s1], 0).astype(jnp.bfloat16))
            tr, ti = turn(row(cs, rv) * rate_v)
            w0 = times(row(vs, ru), row(vs, rv), tr, ti)
            y1, y2 = (row(z1r, rv), row(z1i, rv)), (row(z2r, rv), row(z2i, rv))
            w1, w2 = times(*w0, *y1), times(*w0, *y2)
            w3 = times(*w1, *y2)
            lhs_r.append(jnp.concatenate([w[0] for w in (w0, w1, w2, w3)], 0).astype(jnp.bfloat16))
            lhs_i.append(jnp.concatenate([w[1] for w in (w0, w1, w2, w3)], 0).astype(jnp.bfloat16))
        neg_u = [-x for x in sin_u]
        lhs = jnp.concatenate(lhs_r + lhs_i, 1)
        plus_r, minus_r = jnp.concatenate(cos_u + neg_u, 1), jnp.concatenate(cos_u + sin_u, 1)
        plus_i, minus_i = jnp.concatenate(sin_u + cos_u, 1), jnp.concatenate(neg_u + cos_u, 1)
        rhs = jnp.concatenate([plus_r, minus_r, plus_i, minus_i] * 2, 0)
        out = lax.dot_general(lhs, rhs, (((1,), (1,)), ((), ())), preferred_element_type=jnp.float32)
        for g in range(4):
            v = out[8 * g : 8 * g + 8]
            v = jnp.where(low, v, pltpu.roll(v, 8 - Q2, 0)).astype(jnp.bfloat16)
            for k in range(group):
                d = g * group + k
                place = bit_reverse(d // 2, T // 2)
                ref = send if d % 2 else keep
                ref[place, s] = v[k * Q : k * Q + Q2]
        return carry

    lax.fori_loop(0, L, one, 0, unroll=4)


def images(T, L, counts, offsets, coords, vis):
    Q2 = SUB // T // 2
    half = jax.ShapeDtypeStruct((T // 2, L, Q2, LANES), jnp.bfloat16)
    smem, vmem = pl.BlockSpec(memory_space=pltpu.SMEM), pl.BlockSpec(memory_space=pltpu.VMEM)
    return pl.pallas_call(
        functools.partial(images_kernel, T, L),
        out_shape=(half, half),
        in_specs=[smem, smem, vmem, vmem],
        out_specs=(vmem, vmem),
        scratch_shapes=[pltpu.VMEM((4 * L, LANES), jnp.float32)] * 6,
        name="images",
        **PARAMS,
    )(counts, offsets, coords, vis)


def send_kernel(T, L, B, cap, capx, held, *refs):
    terms, (slots, ids, screens, out, rows, gathered) = refs[:-6], refs[-6:]
    Q2 = SUB // T // 2
    total = terms[0][0].astype(jnp.float32)
    for t in terms[1:]:
        total = total + t[0].astype(jnp.float32)
    rows[...] = total.reshape(L * Q2, LANES)
    hot = (iota((B * capx, L), 0) == slots[...]).astype(jnp.float32).astype(jnp.bfloat16)
    for q in range(Q2):
        x = rows[pl.ds(q, L, stride=Q2), :].astype(jnp.bfloat16)
        moved = jnp.dot(hot, x, preferred_element_type=jnp.float32).astype(jnp.bfloat16)
        gathered[:, LANES * q : LANES * (q + 1)] = moved
    names = ids[...].astype(jnp.bfloat16)
    tail = capx - cap
    F = Q2 * LANES
    mine = screens[...].astype(jnp.float32)
    fill = jnp.zeros((tail - 8, F), jnp.float32) if tail > 8 else None

    def one(o, carry):
        start = pl.multiple_of(o * capx, 8)
        wanted = iota((LANES, L), 0) + o * capx
        own = (wanted == slots[...]).astype(jnp.float32).astype(jnp.bfloat16)
        listed = lax.dot_general(names, own, (((1,), (1,)), ((), ())), preferred_element_type=jnp.float32)
        listed = jnp.concatenate([listed] + [jnp.zeros((8, F - LANES), jnp.float32)], 1)
        extra = jnp.where(iota((8, F), 0) < held, mine, listed)
        if fill is not None:
            extra = jnp.concatenate([extra, fill], 0)
        block = jnp.concatenate([gathered[pl.ds(start, capx), :][:cap].astype(jnp.float32), extra], 0)
        out[o] = block.astype(jnp.bfloat16)
        return carry

    lax.fori_loop(0, B, one, 0)


def send_blocks(T, L, B, cap, capx, held, terms, slots, ids, screens):
    Q2 = SUB // T // 2
    F = Q2 * LANES
    first = pl.BlockSpec((1, L, Q2, LANES), lambda i: (0, 0, 0, 0))
    whole2 = lambda x: pl.BlockSpec(x.shape, lambda i: (0, 0))
    return pl.pallas_call(
        functools.partial(send_kernel, T, L, B, cap, capx, held),
        grid=(1,),
        out_shape=jax.ShapeDtypeStruct((B, capx, F), jnp.bfloat16),
        in_specs=[first] * len(terms) + [whole2(slots), whole2(ids), whole2(screens)],
        out_specs=pl.BlockSpec((B, capx, F), lambda i: (0, 0, 0)),
        scratch_shapes=[pltpu.VMEM((L * Q2, LANES), jnp.float32), pltpu.VMEM((B * capx, F), jnp.bfloat16)],
        name="send",
        **PARAMS,
    )(*terms, slots, ids, screens)


def place_kernel(T, B, cap, capx, held, blocks, col_off, row_off, weights, keep, send, data, gains, hot, spread, rows):
    Q, Q2 = SUB // T, SUB // T // 2
    F = Q2 * LANES
    S = B * cap
    NX = B * 8
    a = lax.axis_index("tm")
    lane_f = iota((8, F), 1)
    part_f = (lane_f // SUB) % 2

    def gather(b, carry):
        data[pl.ds(b * cap, cap), :] = blocks[b, 0:cap, :].astype(jnp.float32)
        x = blocks[b, cap : cap + 8, :].astype(jnp.float32)
        at = pl.ds(pl.multiple_of(b * 8, 8), 8)
        gains[at, 0:F] = jnp.where(part_f == 0, x, pltpu.roll(x, SUB, 1))
        gains[at, F : 2 * F] = jnp.where(part_f == 1, x, pltpu.roll(x, F - SUB, 1))
        same = iota((cap, LANES), 0) == iota((cap, LANES), 1)
        for k in range(2):
            number = x[held + 2 * k : held + 2 * k + 1, 0:LANES] * 8.0 + x[held + 2 * k + 1 : held + 2 * k + 2, 0:LANES]
            number = jnp.sum(jnp.where(same, jnp.broadcast_to(number, (cap, LANES)), 0.0), axis=1, keepdims=True)
            hit = number.astype(jnp.int32) == iota((cap, NX), 1)
            hot[k, pl.ds(b * cap, cap), :] = hit.astype(jnp.float32)
        return carry

    lax.fori_loop(0, B, gather, 0, unroll=min(B, 8))

    hot_p, hot_q = hot[0].astype(jnp.bfloat16), hot[1].astype(jnp.bfloat16)
    lane = iota((1, LANES), 1)
    low, l = lane // (LANES // 2), column_of(lane % SUB)
    away = [(iota((S, LANES), 1) + LANES * v) - col_off[...] for v in range(2)]
    inside = [(w >= 0) & (w < SUB) for w in away]

    def taper(n):
        scaled = (n.astype(jnp.float32) + 0.5 - SUB / 2.0) / (SUB / 2.0)
        return 1.0 - scaled * scaled

    for q in range(Q2):
        at = slice(LANES * q, LANES * (q + 1))
        at_i = slice(F + LANES * q, F + LANES * (q + 1))
        m = T * (low * Q2 + q) + a
        window = taper(m) * taper(l) * (1.0 / (SUB * 16.0))
        tables = [gains[:, at].astype(jnp.bfloat16), gains[:, at_i].astype(jnp.bfloat16)]
        pr, pi = [jnp.dot(hot_p, t, preferred_element_type=jnp.float32) for t in tables]
        qr, qi = [jnp.dot(hot_q, t, preferred_element_type=jnp.float32) for t in tables]
        d = data[:, at] * window
        x = jnp.concatenate([d * (pr * qr + pi * qi), d * (pr * qi - pi * qr)], 1).astype(jnp.bfloat16)
        y = jnp.dot(x, weights[...], preferred_element_type=jnp.float32)
        for h in range(2):
            for c in range(2):
                v = y[:, (h * 2 + c) * LANES : (h * 2 + c + 1) * LANES]
                for half in range(2):
                    spread[pl.ds((q * 2 + h) * S, S), (c * 2 + half) * LANES : (c * 2 + half + 1) * LANES] = jnp.where(
                        inside[half], v, 0.0
                    ).astype(jnp.bfloat16)

    K = 2 * Q2 * S
    chunk = TILE // T
    index = iota((1, K), 1) // S
    m = (T * ((index % 2) * Q2 + index // 2) + a).astype(jnp.float32) * (1.0 / SUB)
    er, ei = turn(iota((SUB, K), 0).astype(jnp.float32) * m)
    for d in range(T):
        for e in range(chunk // SUB):
            r = (a ^ d) * chunk + e * SUB + iota((SUB, K), 0) - row_off[...]
            mask = (r >= 0) & (r < SUB)
            place = (d % 2) * (T // 2) + bit_reverse(d // 2, T // 2)
            at = place * chunk + e * SUB
            rows[at : at + SUB, :] = jnp.where(mask, er, 0.0).astype(jnp.bfloat16)
            rows[TILE + at : TILE + at + SUB, :] = jnp.where(mask, ei, 0.0).astype(jnp.bfloat16)
    both = jnp.dot(rows[...], spread[...], preferred_element_type=jnp.float32)
    u, v = both[:TILE], both[TILE:]
    tile = jnp.concatenate([u[:, :TILE] + v[:, TILE:], u[:, TILE:] - v[:, :TILE]], 1)
    for i in range(T // 2):
        keep[i] = tile[i * chunk : (i + 1) * chunk]
        j = T // 2 + i
        send[i] = tile[j * chunk : (j + 1) * chunk].astype(jnp.bfloat16)


def place_blocks(T, B, cap, capx, held, blocks, col_off, row_off, weights):
    Q2 = SUB // T // 2
    F, S, K = Q2 * LANES, B * cap, 2 * Q2 * B * cap
    vmem = pl.BlockSpec(memory_space=pltpu.VMEM)
    chunk = TILE // T
    return pl.pallas_call(
        functools.partial(place_kernel, T, B, cap, capx, held),
        out_shape=(
            jax.ShapeDtypeStruct((T // 2, chunk, 2 * TILE), jnp.float32),
            jax.ShapeDtypeStruct((T // 2, chunk, 2 * TILE), jnp.bfloat16),
        ),
        in_specs=[vmem] * 4,
        out_specs=(vmem, vmem),
        scratch_shapes=[
            pltpu.VMEM((S, F), jnp.float32),
            pltpu.VMEM((B * 8, 2 * F), jnp.float32),
            pltpu.VMEM((2, S, B * 8), jnp.float32),
            pltpu.VMEM((K, 2 * TILE), jnp.bfloat16),
            pltpu.VMEM((2 * TILE, K), jnp.bfloat16),
        ],
        name="place",
        **PARAMS,
    )(blocks, col_off, row_off, weights)


def transform_weights():
    lam = np.arange(SUB)
    l = np.where(lam < SUB // 2, lam + SUB // 2, SUB - 1 - lam)
    angle = 2.0 * math.pi * (l[:, None] * (np.arange(LANES)[None, :] % SUB) % SUB) / SUB
    cos, sin = np.cos(angle), np.sin(angle)
    out = np.zeros((2, 2, 2, SUB, 2, 2, LANES))
    for h in range(2):
        out[0, h, 0, :, h, 0], out[0, h, 0, :, h, 1] = cos, -sin
        out[0, h, 1, :, h, 0], out[0, h, 1, :, h, 1] = sin, cos
        out[1, h, 1, :, h, 0], out[1, h, 1, :, h, 1] = -cos, sin
        out[1, h, 0, :, h, 0], out[1, h, 0, :, h, 1] = sin, cos
    return jnp.asarray(out.reshape(2 * LANES, 4 * LANES), jnp.float32).astype(jnp.bfloat16)


def halve(T, keep, send):
    swap = lambda x, d: lax.ppermute(x, "tm", [(i, i ^ d) for i in range(T)])
    terms, d = [keep, swap(send, 1)], 2
    while d < T:
        half = T // d // 2
        moving = sum(t[half : 2 * half].astype(jnp.float32) for t in terms).astype(jnp.bfloat16)
        terms.append(swap(moving, d))
        d *= 2
    return terms


def per_device(visibilities, coords, counts, stations, owners, offsets, screens):
    T, B = lax.axis_size("tm"), lax.axis_size("base")
    L, slots = visibilities.shape[1], visibilities.shape[3]
    a, base = lax.axis_index("tm"), lax.axis_index("base")
    Q, Q2 = SUB // T, SUB // T // 2
    F = Q2 * LANES
    held = screens.shape[0]
    cap = -(-max(2, 3 * L // (2 * B)) // 8) * 8
    capx = cap + 8

    def flat(x):
        return x.reshape(L, 2, slots // LANES, LANES).transpose(0, 2, 1, 3).reshape(4 * L, LANES)

    keep, send = images(T, L, counts, offsets.T, flat(coords[0]), flat(visibilities[0]))

    owner = owners[:, 0].reshape(B, L)
    mine = lax.dynamic_slice_in_dim(owner, base, 1, 0)[0]
    order = jnp.arange(L, dtype=jnp.int32)
    earlier = order[:, None] < order[None, :]
    rank = jnp.sum(((mine[:, None] == mine[None, :]) & earlier).astype(jnp.int32), axis=0)
    slot_ids = (mine * capx + rank)[None, :]
    names = jnp.stack([stations[:, 0] // held, stations[:, 0] % held, stations[:, 1] // held, stations[:, 1] % held])
    names = jnp.concatenate([jnp.zeros((8 - 4, L), jnp.float32), names.astype(jnp.float32)], 0)

    pixels = screens.reshape(held, 2, Q, T, SUB)
    pixels = lax.dynamic_slice_in_dim(pixels, a, 1, 3)[:, :, :, 0]
    pixels = jnp.concatenate([pixels[..., SUB // 2 :], pixels[..., : SUB // 2][..., ::-1]], -1)
    pixels = pixels.reshape(held, 2, 2, Q2, SUB).transpose(0, 3, 2, 1, 4).reshape(held, F)
    pixels = jnp.concatenate([pixels, jnp.zeros((8 - held, F), pixels.dtype)], 0)

    to_me = (owner == base)
    before = jnp.sum((to_me[:, :, None] & earlier[None]).astype(jnp.int32), axis=1)
    chosen = to_me[:, None, :] & (before[:, None, :] == jnp.arange(cap, dtype=jnp.int32)[None, :, None])
    offs = offsets.T.reshape(2, B, 1, L)
    slot_offs = jnp.sum(jnp.where(chosen[None], offs, 0), axis=3).reshape(2, B * cap)
    col_off = slot_offs[1][:, None]
    row_off = jnp.tile(slot_offs[0], 2 * Q2)[None, :]

    terms = halve(T, keep, send)
    outgoing = send_blocks(T, L, B, cap, capx, held, terms, slot_ids, names, pixels)
    incoming = lax.all_to_all(outgoing, "base", split_axis=0, concat_axis=0, tiled=True)
    keep, send = place_blocks(T, B, cap, capx, held, incoming, col_off, row_off, transform_weights())
    tile = sum(t[0].astype(jnp.float32) for t in halve(T, keep, send))
    return tile.reshape(1, TILE // T, 2, TILE)


def solution(mesh):
    return jax.shard_map(
        per_device,
        mesh=mesh,
        in_specs=(
            P("tm", "base", None, None),
            P("tm", "base", None, None),
            P("tm", "base"),
            P("base", None),
            P(),
            P(),
            P("base", None, None),
        ),
        out_specs=P("base", "tm", None, None),
        check_vma=False,
    )
```

```python
import functools
import math

import jax
import jax.numpy as jnp
import numpy as np
from jax import lax
from jax.experimental import pallas as pl
from jax.experimental.pallas import tpu as pltpu
from jax.sharding import PartitionSpec as P

SUB = 32
TILE = 256
LANES = 128
SINE = (4.442883014678955, -7.308245658874512, 3.6063544750213623, -0.8461129069328308, 0.10982698202133179)
COSINE = (1.4142135381698608, -6.978850841522217, 5.7394609451293945, -1.8835626224777222, 0.31069815158843994)
PARAMS = dict(compiler_params=pltpu.CompilerParams(vmem_limit_bytes=48 * 1024 * 1024))


def iota(shape, axis):
    return lax.broadcasted_iota(jnp.int32, shape, axis)


def turn(x):
    t = x - jnp.round(x)
    u = t * t
    s = ((((SINE[4] * u + SINE[3]) * u + SINE[2]) * u + SINE[1]) * u + SINE[0]) * t
    c = (((COSINE[4] * u + COSINE[3]) * u + COSINE[2]) * u + COSINE[1]) * u + COSINE[0]
    return 1.0 - s * s, s * c


def times(xr, xi, yr, yi):
    return xr * yr - xi * yi, xr * yi + xi * yr


def bit_reverse(i, size):
    out = 0
    while size > 1:
        out, i, size = out * 2 + i % 2, i // 2, size // 2
    return out


def column_of(lane):
    half = SUB // 2
    return jnp.where(lane < half, lane + half, SUB - 1 - lane)


def images_kernel(T, L, in_counts, in_offsets, in_coords, in_vis, keep, send, z1r, z1i, z2r, z2i, vs, cs, vis, counts, offsets, sems):
    Q, Q2 = SUB // T, SUB // T // 2
    a, base = lax.axis_index("tm"), lax.axis_index("base")
    parts = 2
    span = 4 * L // parts
    numbers = [
        pltpu.make_async_copy(in_counts, counts, sems.at[0]),
        pltpu.make_async_copy(in_offsets.at[:, pl.ds(pl.multiple_of(base * L, LANES), L)], offsets, sems.at[1]),
    ]
    loads = []
    for k in range(parts):
        at = pl.ds(k * span, span)
        loads.append(pltpu.make_async_copy(in_coords.at[at, :], cs.at[at, :], sems.at[2 + 2 * k]))
        loads.append(pltpu.make_async_copy(in_vis.at[at, :], vis.at[at, :], sems.at[3 + 2 * k]))
    for copy in numbers + loads:
        copy.start()
    step1, step2 = T // 4, T // 2
    sign1 = 1 - 2 * ((a // step1) % 2)
    sign2 = 1 - 2 * ((a // step2) % 2)
    sign1f, flip = sign1.astype(jnp.float32), (sign1 * sign2).astype(jnp.float32)

    R = 16
    rho, lane = iota((R, LANES), 0), iota((R, LANES), 1)
    owner, block, part = rho // 4, (rho // 2) % 2, rho % 2
    slot = lane + LANES * block
    rate1 = jnp.where(part == 0, 8.0 / SUB, sign1f * (step1 / SUB))
    flips = jnp.where(part == 0, 1.0, flip)
    crossed = jnp.where(part == 0, -1.0, 1.0)

    def pick(values):
        out = values[-1]
        for k in range(len(values) - 2, -1, -1):
            out = jnp.where(owner == k, values[k], out)
        return out

    def prepare(i, carry):
        rows = pl.ds(pl.multiple_of(i * R, R), R)
        subs = [i * 4 + k for k in range(4)]
        row_off = [offsets[0, s] for s in subs]
        col_off = [offsets[1, s] for s in subs]
        odd = [(r + c) & 1 for r, c in zip(row_off, col_off)]
        signs = [(1 - 2 * o).astype(jnp.float32) for o in odd]
        moved = jnp.where(
            part == 0,
            pick([(c & (SUB - 1)).astype(jnp.float32) for c in col_off]),
            pick([(r & (SUB - 1)).astype(jnp.float32) for r in row_off]),
        )
        c = cs[rows, :] + moved
        cs[rows, :] = c
        r1, i1 = turn(c * rate1)
        z1r[rows, :] = r1
        z1i[rows, :] = i1
        z2r[rows, :] = r1 * r1 - i1 * i1
        z2i[rows, :] = 2.0 * r1 * i1 * flips
        along = jnp.where(part == 0, c, pltpu.roll(c, 1, 0))
        hr, hi = turn(along * (-0.5 / SUB))
        x = vis[rows, :].astype(jnp.float32)
        x = jnp.where(slot < pick([counts[0, s] for s in subs]), x * pick(signs), 0.0)
        other = jnp.where(part == 0, pltpu.roll(x, R - 1, 0), pltpu.roll(x, 1, 0))
        vs[rows, :] = x * hr + other * (hi * crossed)
        return carry

    for copy in numbers:
        copy.wait()
    for k in range(parts):
        loads[2 * k].wait()
        loads[2 * k + 1].wait()
        lax.fori_loop(k * (span // R), (k + 1) * (span // R), prepare, 0, unroll=2)

    rho8 = iota((8, LANES), 0)
    rate_u = (rho8.astype(jnp.float32) + 0.5) * (1.0 / SUB)
    delta, q = rho8 // Q, rho8 % Q
    group = max(1, 8 // Q)
    rate_v = (T * q + (a ^ delta) - SUB // 2).astype(jnp.float32) * (1.0 / SUB)
    low = iota((8, LANES), 1) < LANES // 2

    def row(ref, r):
        return jnp.broadcast_to(ref[pl.ds(r, 1), :], (8, LANES))

    def tables(s):
        lhs_r, lhs_i, cos_u, sin_u = [], [], [], []
        for b in range(2):
            ru = s * 4 + b * 2
            rv = ru + 1
            c0, s0 = turn(row(cs, ru) * rate_u)
            c1, s1 = times(c0, s0, row(z1r, ru), row(z1i, ru))
            cos_u.append(jnp.concatenate([c0, c1], 0).astype(jnp.bfloat16))
            sin_u.append(jnp.concatenate([s0, s1], 0).astype(jnp.bfloat16))
            tr, ti = turn(row(cs, rv) * rate_v)
            w0 = times(row(vs, ru), row(vs, rv), tr, ti)
            y1, y2 = (row(z1r, rv), row(z1i, rv)), (row(z2r, rv), row(z2i, rv))
            w1, w2 = times(*w0, *y1), times(*w0, *y2)
            w3 = times(*w1, *y2)
            lhs_r.append(jnp.concatenate([w[0] for w in (w0, w1, w2, w3)], 0).astype(jnp.bfloat16))
            lhs_i.append(jnp.concatenate([w[1] for w in (w0, w1, w2, w3)], 0).astype(jnp.bfloat16))
        neg_u = [-x for x in sin_u]
        lhs = jnp.concatenate(lhs_r + lhs_i, 1)
        plus_r, minus_r = jnp.concatenate(cos_u + neg_u, 1), jnp.concatenate(cos_u + sin_u, 1)
        plus_i, minus_i = jnp.concatenate(sin_u + cos_u, 1), jnp.concatenate(neg_u + cos_u, 1)
        return lhs, [plus_r, minus_r, plus_i, minus_i]

    def two(p, carry):
        s = 2 * p
        l0, r0 = tables(s)
        l1, r1 = tables(s + 1)
        out = lax.dot_general(
            jnp.concatenate([l0, l1], 0),
            jnp.concatenate(r0 + r1, 0),
            (((1,), (1,)), ((), ())),
            preferred_element_type=jnp.float32,
        )
        for g in range(4):
            x, y = out[8 * g : 8 * g + 8], out[SUB + 8 * g : SUB + 8 * g + 8]
            x = jnp.where(low, x, pltpu.roll(pltpu.roll(x, 8 - Q2, 0), LANES // 2, 1)).astype(jnp.bfloat16)
            y = jnp.where(low, pltpu.roll(y, LANES // 2, 1), pltpu.roll(y, 8 - Q2, 0)).astype(jnp.bfloat16)
            for k in range(group):
                d = g * group + k
                place = bit_reverse(d // 2, T // 2)
                ref = send if d % 2 else keep
                ref[place, s] = x[k * Q : k * Q + Q2]
                ref[place, s + 1] = y[k * Q : k * Q + Q2]
        return carry

    lax.fori_loop(0, L // 2, two, 0, unroll=16)


def images(T, L, counts, offsets, coords, vis):
    Q2 = SUB // T // 2
    half = jax.ShapeDtypeStruct((T // 2, L, Q2, LANES), jnp.bfloat16)
    hbm, vmem = pl.BlockSpec(memory_space=pltpu.HBM), pl.BlockSpec(memory_space=pltpu.VMEM)
    return pl.pallas_call(
        functools.partial(images_kernel, T, L),
        out_shape=(half, half),
        in_specs=[hbm] * 4,
        out_specs=(vmem, vmem),
        scratch_shapes=[pltpu.VMEM((4 * L, LANES), jnp.float32)] * 6
        + [
            pltpu.VMEM((4 * L, LANES), jnp.bfloat16),
            pltpu.SMEM((1, L), jnp.int32),
            pltpu.SMEM((2, L), jnp.int32),
            pltpu.SemaphoreType.DMA((6,)),
        ],
        name="images",
        **PARAMS,
    )(counts, offsets, coords, vis)


def index_kernel(T, L, B, cap, capx, held, owners, stations, screens, hot, extras):
    Q2 = SUB // T // 2
    F = Q2 * LANES
    a, base = lax.axis_index("tm"), lax.axis_index("base")
    mine = jnp.broadcast_to(owners[pl.ds(base, 1), :], (L, L))
    same = (mine == mine.T) & (iota((L, L), 0) < iota((L, L), 1))
    rank = jnp.sum(same.astype(jnp.float32), axis=0, keepdims=True).astype(jnp.int32)
    slots = mine[0:1] * capx + rank
    hot[...] = (iota((B * capx, L), 0) == slots).astype(jnp.float32).astype(jnp.bfloat16)

    lane = iota((1, F), 1)
    m = T * (((lane // (2 * SUB)) % 2) * Q2 + lane // LANES) + a
    pixel = m * SUB + column_of(lane % SUB)
    select = (iota((SUB * SUB, F), 0) == pixel).astype(jnp.float32).astype(jnp.bfloat16)
    x = jnp.concatenate([screens[:, 0, :].astype(jnp.float32), screens[:, 1, :].astype(jnp.float32)], 0)
    x = jnp.dot(x.astype(jnp.bfloat16), select, preferred_element_type=jnp.float32)
    mine_x = jnp.where((lane // SUB) % 2 == 0, x[:held], x[held:])
    mine_x = jnp.concatenate([mine_x, jnp.zeros((8 - held, F), jnp.float32)], 0)

    p, q = stations[0:1, :], stations[1:2, :]
    names = jnp.concatenate([jnp.zeros((4, L), jnp.int32), p // held, p % held, q // held, q % held], 0)
    names = names.astype(jnp.float32).astype(jnp.bfloat16)

    def one(o, carry):
        own = (iota((LANES, L), 0) + o * capx == slots).astype(jnp.float32).astype(jnp.bfloat16)
        listed = lax.dot_general(names, own, (((1,), (1,)), ((), ())), preferred_element_type=jnp.float32)
        listed = jnp.concatenate([listed] + [jnp.zeros((8, F - LANES), jnp.float32)], 1)
        extras[o] = jnp.where(iota((8, F), 0) < 4, mine_x, listed).astype(jnp.bfloat16)
        return carry

    lax.fori_loop(0, B, one, 0, unroll=min(B, 8))


def index_tables(T, L, B, cap, capx, held, owners, stations, screens):
    F = SUB // T // 2 * LANES
    vmem = pl.BlockSpec(memory_space=pltpu.VMEM)
    return pl.pallas_call(
        functools.partial(index_kernel, T, L, B, cap, capx, held),
        out_shape=(
            jax.ShapeDtypeStruct((B * capx, L), jnp.bfloat16),
            jax.ShapeDtypeStruct((B, 8, F), jnp.bfloat16),
        ),
        in_specs=[vmem] * 3,
        out_specs=(vmem, vmem),
        name="index",
        cost_estimate=pl.CostEstimate(flops=10**7, bytes_accessed=10**6, transcendentals=0),
        **PARAMS,
    )(owners, stations, screens)


def send_kernel(T, L, B, cap, capx, *refs):
    terms, (hot, extras, out, rows) = refs[:-4], refs[-4:]
    Q2 = SUB // T // 2
    F = Q2 * LANES
    total = terms[0][0].astype(jnp.float32)
    for t in terms[1:]:
        total = total + t[0].astype(jnp.float32)
    rows[...] = total.reshape(L * Q2, LANES)
    for q in range(Q2):
        x = rows[pl.ds(q, L, stride=Q2), :].astype(jnp.bfloat16)
        moved = jnp.dot(hot[...], x, preferred_element_type=jnp.float32).astype(jnp.bfloat16)
        out[:, :, LANES * q : LANES * (q + 1)] = moved.reshape(B, capx, LANES)
    out[:, cap : cap + 8, :] = extras[...]


def send_blocks(T, L, B, cap, capx, terms, hot, extras):
    Q2 = SUB // T // 2
    F = Q2 * LANES
    first = pl.BlockSpec((1, L, Q2, LANES), lambda i: (0, 0, 0, 0))
    return pl.pallas_call(
        functools.partial(send_kernel, T, L, B, cap, capx),
        grid=(1,),
        out_shape=jax.ShapeDtypeStruct((B, capx, F), jnp.bfloat16),
        in_specs=[first] * len(terms)
        + [pl.BlockSpec((B * capx, L), lambda i: (0, 0)), pl.BlockSpec((B, 8, F), lambda i: (0, 0, 0))],
        out_specs=pl.BlockSpec((B, capx, F), lambda i: (0, 0, 0)),
        scratch_shapes=[pltpu.VMEM((L * Q2, LANES), jnp.float32)],
        name="send",
        **PARAMS,
    )(*terms, hot, extras)


def place_kernel(T, B, cap, capx, held, blocks, col_off, row_off, weights, keep, send, data, gains, hot, spread, rows):
    Q, Q2 = SUB // T, SUB // T // 2
    F = Q2 * LANES
    S = B * cap
    NX = B * 8
    a = lax.axis_index("tm")
    lane_f = iota((8, F), 1)
    part_f = (lane_f // SUB) % 2

    def gather(b, carry):
        data[pl.ds(b * cap, cap), :] = blocks[b, 0:cap, :].astype(jnp.float32)
        x = blocks[b, cap : cap + 8, :].astype(jnp.float32)
        at = pl.ds(pl.multiple_of(b * 8, 8), 8)
        gains[at, 0:F] = jnp.where(part_f == 0, x, pltpu.roll(x, SUB, 1))
        gains[at, F : 2 * F] = jnp.where(part_f == 1, x, pltpu.roll(x, F - SUB, 1))
        same = iota((cap, LANES), 0) == iota((cap, LANES), 1)
        for k in range(2):
            number = x[4 + 2 * k : 5 + 2 * k, 0:LANES] * 8.0 + x[5 + 2 * k : 6 + 2 * k, 0:LANES]
            number = jnp.sum(jnp.where(same, jnp.broadcast_to(number, (cap, LANES)), 0.0), axis=1, keepdims=True)
            hit = number.astype(jnp.int32) == iota((cap, NX), 1)
            hot[k, pl.ds(b * cap, cap), :] = hit.astype(jnp.float32)
        return carry

    lax.fori_loop(0, B, gather, 0, unroll=min(B, 8))

    hot_p, hot_q = hot[0].astype(jnp.bfloat16), hot[1].astype(jnp.bfloat16)
    lane = iota((1, LANES), 1)
    low, l = lane // (LANES // 2), column_of(lane % SUB)
    away = [(iota((S, LANES), 1) + LANES * v) - col_off[...] for v in range(2)]
    inside = [(w >= 0) & (w < SUB) for w in away]

    def taper(n):
        scaled = (n.astype(jnp.float32) + 0.5 - SUB / 2.0) / (SUB / 2.0)
        return 1.0 - scaled * scaled

    for q in range(Q2):
        at = slice(LANES * q, LANES * (q + 1))
        at_i = slice(F + LANES * q, F + LANES * (q + 1))
        m = T * (low * Q2 + q) + a
        window = taper(m) * taper(l) * (1.0 / (SUB * 16.0))
        tables = [gains[:, at].astype(jnp.bfloat16), gains[:, at_i].astype(jnp.bfloat16)]
        pr, pi = [jnp.dot(hot_p, t, preferred_element_type=jnp.float32) for t in tables]
        qr, qi = [jnp.dot(hot_q, t, preferred_element_type=jnp.float32) for t in tables]
        d = data[:, at] * window
        x = jnp.concatenate([d * (pr * qr + pi * qi), d * (pr * qi - pi * qr)], 1).astype(jnp.bfloat16)
        y = jnp.dot(x, weights[...], preferred_element_type=jnp.float32)
        for h in range(2):
            for c in range(2):
                v = y[:, (h * 2 + c) * LANES : (h * 2 + c + 1) * LANES]
                for half in range(2):
                    spread[pl.ds((q * 2 + h) * S, S), (c * 2 + half) * LANES : (c * 2 + half + 1) * LANES] = jnp.where(
                        inside[half], v, 0.0
                    ).astype(jnp.bfloat16)

    K = 2 * Q2 * S
    chunk = TILE // T
    index = iota((1, K), 1) // S
    m = (T * ((index % 2) * Q2 + index // 2) + a).astype(jnp.float32) * (1.0 / SUB)
    er, ei = turn(iota((SUB, K), 0).astype(jnp.float32) * m)
    for d in range(T):
        for e in range(chunk // SUB):
            r = (a ^ d) * chunk + e * SUB + iota((SUB, K), 0) - row_off[...]
            mask = (r >= 0) & (r < SUB)
            place = (d % 2) * (T // 2) + bit_reverse(d // 2, T // 2)
            at = place * chunk + e * SUB
            rows[at : at + SUB, :] = jnp.where(mask, er, 0.0).astype(jnp.bfloat16)
            rows[TILE + at : TILE + at + SUB, :] = jnp.where(mask, ei, 0.0).astype(jnp.bfloat16)
    both = jnp.dot(rows[...], spread[...], preferred_element_type=jnp.float32)
    u, v = both[:TILE], both[TILE:]
    tile = jnp.concatenate([u[:, :TILE] + v[:, TILE:], u[:, TILE:] - v[:, :TILE]], 1)
    for i in range(T // 2):
        keep[i] = tile[i * chunk : (i + 1) * chunk]
        j = T // 2 + i
        send[i] = tile[j * chunk : (j + 1) * chunk].astype(jnp.bfloat16)


def place_blocks(T, B, cap, capx, held, blocks, col_off, row_off, weights):
    Q2 = SUB // T // 2
    F, S, K = Q2 * LANES, B * cap, 2 * Q2 * B * cap
    vmem = pl.BlockSpec(memory_space=pltpu.VMEM)
    chunk = TILE // T
    return pl.pallas_call(
        functools.partial(place_kernel, T, B, cap, capx, held),
        out_shape=(
            jax.ShapeDtypeStruct((T // 2, chunk, 2 * TILE), jnp.float32),
            jax.ShapeDtypeStruct((T // 2, chunk, 2 * TILE), jnp.bfloat16),
        ),
        in_specs=[vmem] * 4,
        out_specs=(vmem, vmem),
        scratch_shapes=[
            pltpu.VMEM((S, F), jnp.float32),
            pltpu.VMEM((B * 8, 2 * F), jnp.float32),
            pltpu.VMEM((2, S, B * 8), jnp.float32),
            pltpu.VMEM((K, 2 * TILE), jnp.bfloat16),
            pltpu.VMEM((2 * TILE, K), jnp.bfloat16),
        ],
        name="place",
        **PARAMS,
    )(blocks, col_off, row_off, weights)


def transform_weights():
    lam = np.arange(SUB)
    l = np.where(lam < SUB // 2, lam + SUB // 2, SUB - 1 - lam)
    angle = 2.0 * math.pi * (l[:, None] * (np.arange(LANES)[None, :] % SUB) % SUB) / SUB
    cos, sin = np.cos(angle), np.sin(angle)
    out = np.zeros((2, 2, 2, SUB, 2, 2, LANES))
    for h in range(2):
        out[0, h, 0, :, h, 0], out[0, h, 0, :, h, 1] = cos, -sin
        out[0, h, 1, :, h, 0], out[0, h, 1, :, h, 1] = sin, cos
        out[1, h, 1, :, h, 0], out[1, h, 1, :, h, 1] = -cos, sin
        out[1, h, 0, :, h, 0], out[1, h, 0, :, h, 1] = sin, cos
    return jnp.asarray(out.reshape(2 * LANES, 4 * LANES), jnp.float32).astype(jnp.bfloat16)


def halve(T, keep, send, late=()):
    swap = lambda x, d: lax.ppermute(x, "tm", [(i, i ^ d) for i in range(T)])
    terms, d = [keep, swap(send, 1)], 2
    while d < T:
        half = T // d // 2
        moving = sum(t[half : 2 * half].astype(jnp.float32) for t in terms).astype(jnp.bfloat16)
        if late and d == 2:
            moving, *late = lax.optimization_barrier((moving, *late))
        terms.append(swap(moving, d))
        d *= 2
    return terms, late


def per_device(visibilities, coords, counts, stations, owners, offsets, screens):
    T, B = lax.axis_size("tm"), lax.axis_size("base")
    L, slots = visibilities.shape[1], visibilities.shape[3]
    base = lax.axis_index("base")
    Q2 = SUB // T // 2
    held = screens.shape[0]
    cap = -(-max(2, 3 * L // (2 * B)) // 8) * 8
    capx = cap + 8

    def flat(x):
        return x.reshape(L, 2, slots // LANES, LANES).transpose(0, 2, 1, 3).reshape(4 * L, LANES)

    keep, send = images(T, L, counts, offsets.T, flat(coords[0]), flat(visibilities[0]))
    terms, late = halve(T, keep, send, (owners, stations, screens))
    owner = late[0][:, 0].reshape(B, L)
    hot, extras = index_tables(T, L, B, cap, capx, held, owner, late[1].T, late[2])
    outgoing = send_blocks(T, L, B, cap, capx, terms, hot, extras)
    outgoing, owners, offsets = lax.optimization_barrier((outgoing, owners, offsets))

    to_me = owners[:, 0].reshape(B, L) == base
    order = jnp.arange(L, dtype=jnp.int32)
    earlier = order[:, None] < order[None, :]
    before = jnp.sum((to_me[:, :, None] & earlier[None]).astype(jnp.int32), axis=1)
    chosen = to_me[:, None, :] & (before[:, None, :] == jnp.arange(cap, dtype=jnp.int32)[None, :, None])
    offs = offsets.T.reshape(2, B, 1, L)
    slot_offs = jnp.sum(jnp.where(chosen[None], offs, 0), axis=3).reshape(2, B * cap)
    col_off = slot_offs[1][:, None]
    row_off = jnp.tile(slot_offs[0], 2 * Q2)[None, :]

    incoming = lax.all_to_all(outgoing, "base", split_axis=0, concat_axis=0, tiled=True)
    keep, send = place_blocks(T, B, cap, capx, held, incoming, col_off, row_off, transform_weights())
    terms, _ = halve(T, keep, send)
    tile = sum(t[0].astype(jnp.float32) for t in terms)
    return tile.reshape(1, TILE // T, 2, TILE)


def solution(mesh):
    return jax.shard_map(
        per_device,
        mesh=mesh,
        in_specs=(
            P("tm", "base", None, None),
            P("tm", "base", None, None),
            P("tm", "base"),
            P("base", None),
            P(),
            P(),
            P("base", None, None),
        ),
        out_specs=P("base", "tm", None, None),
        check_vma=False,
    )
```

```python
import functools
import math

import jax
import jax.numpy as jnp
import numpy as np
from jax import lax
from jax.experimental import pallas as pl
from jax.experimental.pallas import tpu as pltpu
from jax.sharding import PartitionSpec as P

SUB = 32
TILE = 256
LANES = 128
SINE = (4.442883014678955, -7.308245658874512, 3.6063544750213623, -0.8461129069328308, 0.10982698202133179)
COSINE = (1.4142135381698608, -6.978850841522217, 5.7394609451293945, -1.8835626224777222, 0.31069815158843994)
PARAMS = dict(compiler_params=pltpu.CompilerParams(vmem_limit_bytes=48 * 1024 * 1024))


def iota(shape, axis):
    return lax.broadcasted_iota(jnp.int32, shape, axis)


def turn(x):
    t = x - jnp.round(x)
    u = t * t
    s = ((((SINE[4] * u + SINE[3]) * u + SINE[2]) * u + SINE[1]) * u + SINE[0]) * t
    c = (((COSINE[4] * u + COSINE[3]) * u + COSINE[2]) * u + COSINE[1]) * u + COSINE[0]
    return 1.0 - s * s, s * c


def times(xr, xi, yr, yi):
    return xr * yr - xi * yi, xr * yi + xi * yr


def bit_reverse(i, size):
    out = 0
    while size > 1:
        out, i, size = out * 2 + i % 2, i // 2, size // 2
    return out


def column_of(lane):
    half = SUB // 2
    return jnp.where(lane < half, lane + half, SUB - 1 - lane)


def images_kernel(T, L, in_counts, in_offsets, in_coords, in_vis, keep, send, z1r, z1i, z2r, z2i, vs, cs, vis, counts, offsets, sems):
    Q, Q2 = SUB // T, SUB // T // 2
    a, base = lax.axis_index("tm"), lax.axis_index("base")
    parts = 2
    span = 4 * L // parts
    numbers = [
        pltpu.make_async_copy(in_counts, counts, sems.at[0]),
        pltpu.make_async_copy(in_offsets.at[:, pl.ds(pl.multiple_of(base * L, LANES), L)], offsets, sems.at[1]),
    ]
    loads = []
    for k in range(parts):
        at = pl.ds(k * span, span)
        loads.append(pltpu.make_async_copy(in_coords.at[at, :], cs.at[at, :], sems.at[2 + 2 * k]))
        loads.append(pltpu.make_async_copy(in_vis.at[at, :], vis.at[at, :], sems.at[3 + 2 * k]))
    for copy in numbers + loads:
        copy.start()
    step1, step2 = T // 4, T // 2
    sign1 = 1 - 2 * ((a // step1) % 2)
    sign2 = 1 - 2 * ((a // step2) % 2)
    sign1f, flip = sign1.astype(jnp.float32), (sign1 * sign2).astype(jnp.float32)

    R = 16
    rho, lane = iota((R, LANES), 0), iota((R, LANES), 1)
    owner, block, part = rho // 4, (rho // 2) % 2, rho % 2
    slot = lane + LANES * block
    rate1 = jnp.where(part == 0, 8.0 / SUB, sign1f * (step1 / SUB))
    flips = jnp.where(part == 0, 1.0, flip)
    crossed = jnp.where(part == 0, -1.0, 1.0)

    def pick(values):
        out = values[-1]
        for k in range(len(values) - 2, -1, -1):
            out = jnp.where(owner == k, values[k], out)
        return out

    def prepare(i, carry):
        rows = pl.ds(pl.multiple_of(i * R, R), R)
        subs = [i * 4 + k for k in range(4)]
        row_off = [offsets[0, s] for s in subs]
        col_off = [offsets[1, s] for s in subs]
        odd = [(r + c) & 1 for r, c in zip(row_off, col_off)]
        signs = [(1 - 2 * o).astype(jnp.float32) for o in odd]
        moved = jnp.where(
            part == 0,
            pick([(c & (SUB - 1)).astype(jnp.float32) for c in col_off]),
            pick([(r & (SUB - 1)).astype(jnp.float32) for r in row_off]),
        )
        c = cs[rows, :] + moved
        cs[rows, :] = c
        r1, i1 = turn(c * rate1)
        z1r[rows, :] = r1
        z1i[rows, :] = i1
        z2r[rows, :] = r1 * r1 - i1 * i1
        z2i[rows, :] = 2.0 * r1 * i1 * flips
        along = jnp.where(part == 0, c, pltpu.roll(c, 1, 0))
        hr, hi = turn(along * (-0.5 / SUB))
        x = vis[rows, :].astype(jnp.float32)
        x = jnp.where(slot < pick([counts[0, s] for s in subs]), x * pick(signs), 0.0)
        other = jnp.where(part == 0, pltpu.roll(x, R - 1, 0), pltpu.roll(x, 1, 0))
        vs[rows, :] = x * hr + other * (hi * crossed)
        return carry

    for copy in numbers:
        copy.wait()
    for k in range(parts):
        loads[2 * k].wait()
        loads[2 * k + 1].wait()
        lax.fori_loop(k * (span // R), (k + 1) * (span // R), prepare, 0, unroll=2)

    rho8 = iota((8, LANES), 0)
    rate_u = (rho8.astype(jnp.float32) + 0.5) * (1.0 / SUB)
    delta, q = rho8 // Q, rho8 % Q
    group = max(1, 8 // Q)
    rate_v = (T * q + (a ^ delta) - SUB // 2).astype(jnp.float32) * (1.0 / SUB)
    low = iota((8, LANES), 1) < LANES // 2

    def row(ref, r):
        return jnp.broadcast_to(ref[pl.ds(r, 1), :], (8, LANES))

    def tables(s):
        lhs_r, lhs_i, cos_u, sin_u = [], [], [], []
        for b in range(2):
            ru = s * 4 + b * 2
            rv = ru + 1
            c0, s0 = turn(row(cs, ru) * rate_u)
            c1, s1 = times(c0, s0, row(z1r, ru), row(z1i, ru))
            cos_u.append(jnp.concatenate([c0, c1], 0).astype(jnp.bfloat16))
            sin_u.append(jnp.concatenate([s0, s1], 0).astype(jnp.bfloat16))
            tr, ti = turn(row(cs, rv) * rate_v)
            w0 = times(row(vs, ru), row(vs, rv), tr, ti)
            y1, y2 = (row(z1r, rv), row(z1i, rv)), (row(z2r, rv), row(z2i, rv))
            w1, w2 = times(*w0, *y1), times(*w0, *y2)
            w3 = times(*w1, *y2)
            lhs_r.append(jnp.concatenate([w[0] for w in (w0, w1, w2, w3)], 0).astype(jnp.bfloat16))
            lhs_i.append(jnp.concatenate([w[1] for w in (w0, w1, w2, w3)], 0).astype(jnp.bfloat16))
        neg_u = [-x for x in sin_u]
        lhs = jnp.concatenate(lhs_r + lhs_i, 1)
        plus_r, minus_r = jnp.concatenate(cos_u + neg_u, 1), jnp.concatenate(cos_u + sin_u, 1)
        plus_i, minus_i = jnp.concatenate(sin_u + cos_u, 1), jnp.concatenate(neg_u + cos_u, 1)
        return lhs, [plus_r, minus_r, plus_i, minus_i]

    def two(p, carry):
        s = 2 * p
        l0, r0 = tables(s)
        l1, r1 = tables(s + 1)
        out = lax.dot_general(
            jnp.concatenate([l0, l1], 0),
            jnp.concatenate(r0 + r1, 0),
            (((1,), (1,)), ((), ())),
            preferred_element_type=jnp.float32,
        )
        for g in range(4):
            x, y = out[8 * g : 8 * g + 8], out[SUB + 8 * g : SUB + 8 * g + 8]
            x = jnp.where(low, x, pltpu.roll(pltpu.roll(x, 8 - Q2, 0), LANES // 2, 1)).astype(jnp.bfloat16)
            y = jnp.where(low, pltpu.roll(y, LANES // 2, 1), pltpu.roll(y, 8 - Q2, 0)).astype(jnp.bfloat16)
            for k in range(group):
                d = g * group + k
                place = bit_reverse(d // 2, T // 2)
                ref = send if d % 2 else keep
                ref[place, s] = x[k * Q : k * Q + Q2]
                ref[place, s + 1] = y[k * Q : k * Q + Q2]
        return carry

    lax.fori_loop(0, L // 2, two, 0, unroll=32)


def images(T, L, counts, offsets, coords, vis):
    Q2 = SUB // T // 2
    half = jax.ShapeDtypeStruct((T // 2, L, Q2, LANES), jnp.bfloat16)
    hbm, vmem = pl.BlockSpec(memory_space=pltpu.HBM), pl.BlockSpec(memory_space=pltpu.VMEM)
    return pl.pallas_call(
        functools.partial(images_kernel, T, L),
        out_shape=(half, half),
        in_specs=[hbm] * 4,
        out_specs=(vmem, vmem),
        scratch_shapes=[pltpu.VMEM((4 * L, LANES), jnp.float32)] * 6
        + [
            pltpu.VMEM((4 * L, LANES), jnp.bfloat16),
            pltpu.SMEM((1, L), jnp.int32),
            pltpu.SMEM((2, L), jnp.int32),
            pltpu.SemaphoreType.DMA((6,)),
        ],
        name="images",
        **PARAMS,
    )(*[pltpu.with_memory_space_constraint(x, pltpu.HBM) for x in (counts, offsets, coords, vis)])


def index_kernel(T, L, B, cap, capx, held, owners, stations, screens, hot, extras):
    Q2 = SUB // T // 2
    F = Q2 * LANES
    a, base = lax.axis_index("tm"), lax.axis_index("base")
    mine = jnp.broadcast_to(owners[pl.ds(base, 1), :], (L, L))
    same = (mine == mine.T) & (iota((L, L), 0) < iota((L, L), 1))
    rank = jnp.sum(same.astype(jnp.float32), axis=0, keepdims=True).astype(jnp.int32)
    slots = mine[0:1] * capx + rank
    hot[...] = (iota((B * capx, L), 0) == slots).astype(jnp.float32).astype(jnp.bfloat16)

    lane = iota((1, F), 1)
    m = T * (((lane // (2 * SUB)) % 2) * Q2 + lane // LANES) + a
    pixel = m * SUB + column_of(lane % SUB)
    select = (iota((SUB * SUB, F), 0) == pixel).astype(jnp.float32).astype(jnp.bfloat16)
    x = jnp.concatenate([screens[:, 0, :].astype(jnp.float32), screens[:, 1, :].astype(jnp.float32)], 0)
    x = jnp.dot(x.astype(jnp.bfloat16), select, preferred_element_type=jnp.float32)
    mine_x = jnp.where((lane // SUB) % 2 == 0, x[:held], x[held:])
    mine_x = jnp.concatenate([mine_x, jnp.zeros((8 - held, F), jnp.float32)], 0)

    p, q = stations[0:1, :], stations[1:2, :]
    names = jnp.concatenate([jnp.zeros((4, L), jnp.int32), p // held, p % held, q // held, q % held], 0)
    names = names.astype(jnp.float32).astype(jnp.bfloat16)

    def one(o, carry):
        own = (iota((LANES, L), 0) + o * capx == slots).astype(jnp.float32).astype(jnp.bfloat16)
        listed = lax.dot_general(names, own, (((1,), (1,)), ((), ())), preferred_element_type=jnp.float32)
        listed = jnp.concatenate([listed] + [jnp.zeros((8, F - LANES), jnp.float32)], 1)
        extras[o] = jnp.where(iota((8, F), 0) < 4, mine_x, listed).astype(jnp.bfloat16)
        return carry

    lax.fori_loop(0, B, one, 0, unroll=min(B, 8))


def index_tables(T, L, B, cap, capx, held, owners, stations, screens):
    F = SUB // T // 2 * LANES
    vmem = pl.BlockSpec(memory_space=pltpu.VMEM)
    return pl.pallas_call(
        functools.partial(index_kernel, T, L, B, cap, capx, held),
        out_shape=(
            jax.ShapeDtypeStruct((B * capx, L), jnp.bfloat16),
            jax.ShapeDtypeStruct((B, 8, F), jnp.bfloat16),
        ),
        in_specs=[vmem] * 3,
        out_specs=(vmem, vmem),
        name="index",
        cost_estimate=pl.CostEstimate(flops=10**7, bytes_accessed=10**6, transcendentals=0),
        **PARAMS,
    )(owners, stations, screens)


def send_kernel(T, L, B, cap, capx, *refs):
    terms, (hot, extras, out, rows) = refs[:-4], refs[-4:]
    Q2 = SUB // T // 2
    F = Q2 * LANES
    total = terms[0][0].astype(jnp.float32)
    for t in terms[1:]:
        total = total + t[0].astype(jnp.float32)
    rows[...] = total.reshape(L * Q2, LANES)
    for q in range(Q2):
        x = rows[pl.ds(q, L, stride=Q2), :].astype(jnp.bfloat16)
        moved = jnp.dot(hot[...], x, preferred_element_type=jnp.float32).astype(jnp.bfloat16)
        out[:, :, LANES * q : LANES * (q + 1)] = moved.reshape(B, capx, LANES)
    out[:, cap : cap + 8, :] = extras[...]


def send_blocks(T, L, B, cap, capx, terms, hot, extras):
    Q2 = SUB // T // 2
    F = Q2 * LANES
    vmem = pl.BlockSpec(memory_space=pltpu.VMEM)
    return pl.pallas_call(
        functools.partial(send_kernel, T, L, B, cap, capx),
        out_shape=jax.ShapeDtypeStruct((B, capx, F), jnp.bfloat16),
        in_specs=[vmem] * (len(terms) + 2),
        out_specs=vmem,
        scratch_shapes=[pltpu.VMEM((L * Q2, LANES), jnp.float32)],
        name="send",
        **PARAMS,
    )(*terms, hot, extras)


def rows_kernel(T, S, row_off, rows):
    Q2 = SUB // T // 2
    K = 2 * Q2 * S
    chunk, half = TILE // T, TILE // 2
    a = lax.axis_index("tm")
    index = iota((1, K), 1) // S
    m = (T * ((index % 2) * Q2 + index // 2) + a).astype(jnp.float32) * (1.0 / SUB)
    er, ei = turn(iota((SUB, K), 0).astype(jnp.float32) * m)
    for d in range(T):
        for e in range(chunk // SUB):
            r = (a ^ d) * chunk + e * SUB + iota((SUB, K), 0) - row_off[...]
            mask = (r >= 0) & (r < SUB)
            at = bit_reverse(d // 2, T // 2) * chunk + e * SUB
            rows[d % 2, at : at + SUB, :] = jnp.where(mask, er, 0.0).astype(jnp.bfloat16)
            rows[d % 2, half + at : half + at + SUB, :] = jnp.where(mask, ei, 0.0).astype(jnp.bfloat16)


def row_tables(T, S, row_off):
    K = SUB // T * S
    vmem = pl.BlockSpec(memory_space=pltpu.VMEM)
    return pl.pallas_call(
        functools.partial(rows_kernel, T, S),
        out_shape=jax.ShapeDtypeStruct((2, TILE, K), jnp.bfloat16),
        in_specs=[vmem],
        out_specs=vmem,
        name="rows",
        cost_estimate=pl.CostEstimate(flops=10**7, bytes_accessed=10**6, transcendentals=0),
        **PARAMS,
    )(row_off)


def tile_part(T, rows, spread):
    both = jnp.dot(rows, spread, preferred_element_type=jnp.float32)
    u, v = both[: TILE // 2], both[TILE // 2 :]
    tile = jnp.concatenate([u[:, :TILE] + v[:, TILE:], u[:, TILE:] - v[:, :TILE]], 1)
    return tile.reshape(T // 2, TILE // T, 2 * TILE)


def place_kernel(T, B, cap, capx, held, blocks, col_off, rows, weights, spread, send, data, gains, hot):
    Q, Q2 = SUB // T, SUB // T // 2
    F = Q2 * LANES
    S = B * cap
    NX = B * 8
    a = lax.axis_index("tm")
    lane_f = iota((8, F), 1)
    part_f = (lane_f // SUB) % 2

    def gather(b, carry):
        data[pl.ds(b * cap, cap), :] = blocks[b, 0:cap, :].astype(jnp.float32)
        x = blocks[b, cap : cap + 8, :].astype(jnp.float32)
        at = pl.ds(pl.multiple_of(b * 8, 8), 8)
        gains[at, 0:F] = jnp.where(part_f == 0, x, pltpu.roll(x, SUB, 1))
        gains[at, F : 2 * F] = jnp.where(part_f == 1, x, pltpu.roll(x, F - SUB, 1))
        same = iota((cap, LANES), 0) == iota((cap, LANES), 1)
        for k in range(2):
            number = x[4 + 2 * k : 5 + 2 * k, 0:LANES] * 8.0 + x[5 + 2 * k : 6 + 2 * k, 0:LANES]
            number = jnp.sum(jnp.where(same, jnp.broadcast_to(number, (cap, LANES)), 0.0), axis=1, keepdims=True)
            hit = number.astype(jnp.int32) == iota((cap, NX), 1)
            hot[k, pl.ds(b * cap, cap), :] = hit.astype(jnp.float32)
        return carry

    lax.fori_loop(0, B, gather, 0, unroll=min(B, 8))

    hot_p, hot_q = hot[0].astype(jnp.bfloat16), hot[1].astype(jnp.bfloat16)
    lane = iota((1, LANES), 1)
    low, l = lane // (LANES // 2), column_of(lane % SUB)
    away = [(iota((S, LANES), 1) + LANES * v) - col_off[...] for v in range(2)]
    inside = [(w >= 0) & (w < SUB) for w in away]

    def taper(n):
        scaled = (n.astype(jnp.float32) + 0.5 - SUB / 2.0) / (SUB / 2.0)
        return 1.0 - scaled * scaled

    for q in range(Q2):
        at = slice(LANES * q, LANES * (q + 1))
        at_i = slice(F + LANES * q, F + LANES * (q + 1))
        m = T * (low * Q2 + q) + a
        window = taper(m) * taper(l) * (1.0 / (SUB * 16.0))
        tables = [gains[:, at].astype(jnp.bfloat16), gains[:, at_i].astype(jnp.bfloat16)]
        pr, pi = [jnp.dot(hot_p, t, preferred_element_type=jnp.float32) for t in tables]
        qr, qi = [jnp.dot(hot_q, t, preferred_element_type=jnp.float32) for t in tables]
        d = data[:, at] * window
        x = jnp.concatenate([d * (pr * qr + pi * qi), d * (pr * qi - pi * qr)], 1).astype(jnp.bfloat16)
        y = jnp.dot(x, weights[...], preferred_element_type=jnp.float32)
        for h in range(2):
            for c in range(2):
                v = y[:, (h * 2 + c) * LANES : (h * 2 + c + 1) * LANES]
                for half in range(2):
                    spread[pl.ds((q * 2 + h) * S, S), (c * 2 + half) * LANES : (c * 2 + half + 1) * LANES] = jnp.where(
                        inside[half], v, 0.0
                    ).astype(jnp.bfloat16)

    send[...] = tile_part(T, rows[1], spread[...]).astype(jnp.bfloat16)


def place_blocks(T, B, cap, capx, held, blocks, col_off, rows, weights):
    Q2 = SUB // T // 2
    F, S, K = Q2 * LANES, B * cap, 2 * Q2 * B * cap
    vmem = pl.BlockSpec(memory_space=pltpu.VMEM)
    return pl.pallas_call(
        functools.partial(place_kernel, T, B, cap, capx, held),
        out_shape=(
            jax.ShapeDtypeStruct((K, 2 * TILE), jnp.bfloat16),
            jax.ShapeDtypeStruct((T // 2, TILE // T, 2 * TILE), jnp.bfloat16),
        ),
        in_specs=[vmem] * 4,
        out_specs=(vmem, vmem),
        scratch_shapes=[
            pltpu.VMEM((S, F), jnp.float32),
            pltpu.VMEM((B * 8, 2 * F), jnp.float32),
            pltpu.VMEM((2, S, B * 8), jnp.float32),
        ],
        name="place",
        **PARAMS,
    )(blocks, col_off, rows, weights)


def keep_kernel(T, rows, spread, keep):
    keep[...] = tile_part(T, rows[0], spread[...])


def kept_rows(T, rows, spread):
    vmem = pl.BlockSpec(memory_space=pltpu.VMEM)
    return pl.pallas_call(
        functools.partial(keep_kernel, T),
        out_shape=jax.ShapeDtypeStruct((T // 2, TILE // T, 2 * TILE), jnp.float32),
        in_specs=[vmem] * 2,
        out_specs=vmem,
        name="keep",
        cost_estimate=pl.CostEstimate(flops=10**8, bytes_accessed=10**6, transcendentals=0),
        **PARAMS,
    )(rows, spread)


def transform_weights():
    lam = np.arange(SUB)
    l = np.where(lam < SUB // 2, lam + SUB // 2, SUB - 1 - lam)
    angle = 2.0 * math.pi * (l[:, None] * (np.arange(LANES)[None, :] % SUB) % SUB) / SUB
    cos, sin = np.cos(angle), np.sin(angle)
    out = np.zeros((2, 2, 2, SUB, 2, 2, LANES))
    for h in range(2):
        out[0, h, 0, :, h, 0], out[0, h, 0, :, h, 1] = cos, -sin
        out[0, h, 1, :, h, 0], out[0, h, 1, :, h, 1] = sin, cos
        out[1, h, 1, :, h, 0], out[1, h, 1, :, h, 1] = -cos, sin
        out[1, h, 0, :, h, 0], out[1, h, 0, :, h, 1] = sin, cos
    return jnp.asarray(out.reshape(2 * LANES, 4 * LANES), jnp.float32).astype(jnp.bfloat16)


def halve(T, keep, send, late=()):
    swap = lambda x, d: lax.ppermute(x, "tm", [(i, i ^ d) for i in range(T)])
    terms, d = [keep, swap(send, 1)], 2
    while d < T:
        half = T // d // 2
        moving = sum(t[half : 2 * half].astype(jnp.float32) for t in terms).astype(jnp.bfloat16)
        if late and d == 2:
            moving, *late = lax.optimization_barrier((moving, *late))
        terms.append(swap(moving, d))
        d *= 2
    return terms, late


def per_device(visibilities, coords, counts, stations, owners, offsets, screens):
    T, B = lax.axis_size("tm"), lax.axis_size("base")
    L, slots = visibilities.shape[1], visibilities.shape[3]
    base = lax.axis_index("base")
    Q2 = SUB // T // 2
    held = screens.shape[0]
    cap = -(-max(2, 3 * L // (2 * B)) // 8) * 8
    capx = cap + 8

    def flat(x):
        return x.reshape(L, 2, slots // LANES, LANES).transpose(0, 2, 1, 3).reshape(4 * L, LANES)

    keep, send = images(T, L, counts, offsets.T, flat(coords[0]), flat(visibilities[0]))
    terms, late = halve(T, keep, send, (owners, stations, screens))
    owner = late[0][:, 0].reshape(B, L)
    hot, extras = index_tables(T, L, B, cap, capx, held, owner, late[1].T, late[2])
    outgoing = send_blocks(T, L, B, cap, capx, terms, hot, extras)
    outgoing, owners, offsets = lax.optimization_barrier((outgoing, owners, offsets))

    to_me = owners[:, 0].reshape(B, L) == base
    order = jnp.arange(L, dtype=jnp.int32)
    earlier = order[:, None] < order[None, :]
    before = jnp.sum((to_me[:, :, None] & earlier[None]).astype(jnp.int32), axis=1)
    chosen = to_me[:, None, :] & (before[:, None, :] == jnp.arange(cap, dtype=jnp.int32)[None, :, None])
    offs = offsets.T.reshape(2, B, 1, L)
    slot_offs = jnp.sum(jnp.where(chosen[None], offs, 0), axis=3).reshape(2, B * cap)
    col_off = slot_offs[1][:, None]
    row_off = jnp.tile(slot_offs[0], 2 * Q2)[None, :]

    incoming = lax.all_to_all(outgoing, "base", split_axis=0, concat_axis=0, tiled=True)
    rows = row_tables(T, B * cap, row_off)
    spread, send = place_blocks(T, B, cap, capx, held, incoming, col_off, rows, transform_weights())
    terms, _ = halve(T, kept_rows(T, rows, spread), send)
    tile = sum(t[0].astype(jnp.float32) for t in terms)
    return tile.reshape(1, TILE // T, 2, TILE)


def solution(mesh):
    return jax.shard_map(
        per_device,
        mesh=mesh,
        in_specs=(
            P("tm", "base", None, None),
            P("tm", "base", None, None),
            P("tm", "base"),
            P("base", None),
            P(),
            P(),
            P("base", None, None),
        ),
        out_specs=P("base", "tm", None, None),
        check_vma=False,
    )
```

```python
import functools
import math

import jax
import jax.numpy as jnp
import numpy as np
from jax import lax
from jax.experimental import pallas as pl
from jax.experimental.pallas import tpu as pltpu
from jax.sharding import PartitionSpec as P

SUB = 32
TILE = 256
LANES = 128
GROUP = 32
SINE = (4.442883014678955, -7.308245658874512, 3.6063544750213623, -0.8461129069328308, 0.10982698202133179)
COSINE = (1.4142135381698608, -6.978850841522217, 5.7394609451293945, -1.8835626224777222, 0.31069815158843994)
PARAMS = dict(compiler_params=pltpu.CompilerParams(vmem_limit_bytes=48 * 1024 * 1024))


def iota(shape, axis):
    return lax.broadcasted_iota(jnp.int32, shape, axis)


def turn(x):
    t = x - jnp.round(x)
    u = t * t
    s = ((((SINE[4] * u + SINE[3]) * u + SINE[2]) * u + SINE[1]) * u + SINE[0]) * t
    c = (((COSINE[4] * u + COSINE[3]) * u + COSINE[2]) * u + COSINE[1]) * u + COSINE[0]
    return 1.0 - s * s, s * c


def times(xr, xi, yr, yi):
    return xr * yr - xi * yi, xr * yi + xi * yr


def bit_reverse(i, size):
    out = 0
    while size > 1:
        out, i, size = out * 2 + i % 2, i // 2, size // 2
    return out


def column_of(lane):
    half = SUB // 2
    return jnp.where(lane < half, lane + half, SUB - 1 - lane)


def images_kernel(T, L, G, in_counts, in_offsets, in_coords, in_vis, keep, send, cs, vs, vis, counts, offsets, sems, *tables):
    Q, Q2 = SUB // T, SUB // T // 2
    half_u = SUB // 2
    a, base = lax.axis_index("tm"), lax.axis_index("base")
    parts = 2
    span = 4 * L // parts
    numbers = [
        pltpu.make_async_copy(in_counts, counts, sems.at[0]),
        pltpu.make_async_copy(in_offsets.at[:, pl.ds(pl.multiple_of(base * L, LANES), L)], offsets, sems.at[1]),
    ]
    loads = []
    for k in range(parts):
        at = pl.ds(k * span, span)
        loads.append(pltpu.make_async_copy(in_coords.at[at, :], cs.at[at, :], sems.at[2 + 2 * k]))
        loads.append(pltpu.make_async_copy(in_vis.at[at, :], vis.at[at, :], sems.at[3 + 2 * k]))
    for copy in numbers + loads:
        copy.start()

    row8, lane8 = iota((8, LANES), 0), iota((8, LANES), 1)
    owner, slot = row8 // 2, lane8 + LANES * (row8 % 2)
    low = lane8 < LANES // 2

    def pick(values):
        out = values[-1]
        for k in range(len(values) - 2, -1, -1):
            out = jnp.where(owner == k, values[k], out)
        return out

    def powers(first, n, place_c, place_v, lr, li, uc, us):
        subs = [first + 4 * n + k for k in range(4)]
        even, odd = pl.ds(16 * n, 8, stride=2), pl.ds(16 * n + 1, 8, stride=2)
        row_off, col_off = [offsets[0, k] for k in subs], [offsets[1, k] for k in subs]
        signs = [(1 - 2 * ((r + c) & 1)).astype(jnp.float32) for r, c in zip(row_off, col_off)]
        cu = place_c[even, :] + pick([(c & (SUB - 1)).astype(jnp.float32) for c in col_off])
        cv = place_c[odd, :] + pick([(r & (SUB - 1)).astype(jnp.float32) for r in row_off])
        scale = jnp.where(slot < pick([counts[0, k] for k in subs]), pick(signs), 0.0)
        vr, vi = place_v[even, :] * scale, place_v[odd, :] * scale

        half = turn(cu * (0.5 / SUB))
        step = times(*half, *half)
        e = half
        for k in range(half_u):
            uc[(n * half_u + k) * 8 : (n * half_u + k) * 8 + 8, :] = e[0]
            us[(n * half_u + k) * 8 : (n * half_u + k) * 8 + 8, :] = e[1]
            if k + 1 < half_u:
                e = times(*e, *step)
        y1 = turn(cv * (1.0 / SUB))
        y2 = times(*y1, *y1)
        y4 = times(*y2, *y2)
        w0 = times(vr, vi, *turn(cv * -0.5 - cu * (0.5 / SUB)))
        w1 = times(*w0, *y1)
        chain = [w0, w1, times(*w0, *y2), times(*w1, *y2)]
        for m in range(SUB):
            w = chain[m % 4]
            at = pl.multiple_of((n * SUB + ((m % T) ^ a) * Q + m // T) * 8, 8)
            lr[pl.ds(at, 8), :] = w[0]
            li[pl.ds(at, 8), :] = w[1]
            if m + 4 < SUB:
                chain[m % 4] = times(*w, *y4)

    def sides(n, lr, li, uc, us):
        lhs, cos_u, sin_u = [], [], []
        for ref in (lr, li):
            lhs += [ref[pl.ds((n // 4) * SUB * 8 + (2 * n + b) % 8, SUB, stride=8), :].astype(jnp.bfloat16) for b in range(2)]
        for b in range(2):
            at = pl.ds((n // 4) * half_u * 8 + (2 * n + b) % 8, half_u, stride=8)
            cos_u.append(uc[at, :].astype(jnp.bfloat16))
            sin_u.append(us[at, :].astype(jnp.bfloat16))
        neg_u = [-x for x in sin_u]
        rhs = [cos_u + neg_u, cos_u + sin_u, sin_u + cos_u, neg_u + cos_u]
        return jnp.concatenate(lhs, 1), [jnp.concatenate(r, 1) for r in rhs]

    def products(keep, send, n, *refs):
        s = 2 * n
        (l0, r0), (l1, r1) = sides(2 * n, *refs), sides(2 * n + 1, *refs)
        out = lax.dot_general(
            jnp.concatenate([l0, l1], 0),
            jnp.concatenate(r0 + r1, 0),
            (((1,), (1,)), ((), ())),
            preferred_element_type=jnp.float32,
        )
        group = max(1, 8 // Q)
        for g in range(4):
            x, y = out[8 * g : 8 * g + 8], out[SUB + 8 * g : SUB + 8 * g + 8]
            x = jnp.where(low, x, pltpu.roll(pltpu.roll(x, 8 - Q2, 0), LANES // 2, 1)).astype(jnp.bfloat16)
            y = jnp.where(low, pltpu.roll(y, LANES // 2, 1), pltpu.roll(y, 8 - Q2, 0)).astype(jnp.bfloat16)
            for k in range(group):
                d = g * group + k
                place = bit_reverse(d // 2, T // 2)
                ref = send if d % 2 else keep
                ref[place, s] = x[k * Q : k * Q + Q2]
                ref[place, s + 1] = y[k * Q : k * Q + Q2]

    for copy in numbers:
        copy.wait()
    sides_of = [tables[0:4], tables[4:8]]
    total = L // G

    def arrive(k):
        loads[2 * k].wait()
        loads[2 * k + 1].wait()
        vs[k * span : (k + 1) * span, :] = vis[k * span : (k + 1) * span, :].astype(jnp.float32)

    def make(i, side):
        at = pl.ds(pl.multiple_of(i * G * 4, 8), G * 4)
        for n in range(G // 4):
            powers(i * G, n, cs.at[at, :], vs.at[at, :], *sides_of[side])

    def use(i, side):
        at = pl.ds(i * G, G)
        for n in range(G // 2):
            products(keep.at[:, at], send.at[:, at], n, *sides_of[side])

    def step(j, carry):
        make(2 * j + 1, 1)
        use(2 * j, 0)
        make(2 * j + 2, 0)
        use(2 * j + 1, 1)
        return carry

    arrive(0)
    make(0, 0)
    for k in range(1, parts):
        arrive(k)
    lax.fori_loop(0, total // 2 - 1, step, 0)
    make(total - 1, 1)
    use(total - 2, 0)
    use(total - 1, 1)


def images(T, L, counts, offsets, coords, vis):
    Q2, G = SUB // T // 2, GROUP
    half = jax.ShapeDtypeStruct((T // 2, L, Q2, LANES), jnp.bfloat16)
    hbm, vmem = pl.BlockSpec(memory_space=pltpu.HBM), pl.BlockSpec(memory_space=pltpu.VMEM)
    table = lambda n: pltpu.VMEM((2 * G * n, LANES), jnp.float32)
    return pl.pallas_call(
        functools.partial(images_kernel, T, L, G),
        out_shape=(half, half),
        in_specs=[hbm] * 4,
        out_specs=(vmem, vmem),
        scratch_shapes=[pltpu.VMEM((4 * L, LANES), jnp.float32)] * 2
        + [
            pltpu.VMEM((4 * L, LANES), jnp.bfloat16),
            pltpu.SMEM((1, L), jnp.int32),
            pltpu.SMEM((2, L), jnp.int32),
            pltpu.SemaphoreType.DMA((6,)),
        ]
        + [table(SUB), table(SUB), table(SUB // 2), table(SUB // 2)] * 2,
        name="images",
        **PARAMS,
    )(*[pltpu.with_memory_space_constraint(x, pltpu.HBM) for x in (counts, offsets, coords, vis)])


def index_kernel(T, L, B, cap, capx, held, owners, stations, screens, hot, extras):
    Q2 = SUB // T // 2
    F = Q2 * LANES
    a, base = lax.axis_index("tm"), lax.axis_index("base")
    mine = jnp.broadcast_to(owners[pl.ds(base, 1), :], (L, L))
    same = (mine == mine.T) & (iota((L, L), 0) < iota((L, L), 1))
    rank = jnp.sum(same.astype(jnp.float32), axis=0, keepdims=True).astype(jnp.int32)
    slots = mine[0:1] * capx + rank
    hot[...] = (iota((B * capx, L), 0) == slots).astype(jnp.float32).astype(jnp.bfloat16)

    lane = iota((1, F), 1)
    m = T * (((lane // (2 * SUB)) % 2) * Q2 + lane // LANES) + a
    pixel = m * SUB + column_of(lane % SUB)
    select = (iota((SUB * SUB, F), 0) == pixel).astype(jnp.float32).astype(jnp.bfloat16)
    x = jnp.concatenate([screens[:, 0, :].astype(jnp.float32), screens[:, 1, :].astype(jnp.float32)], 0)
    x = jnp.dot(x.astype(jnp.bfloat16), select, preferred_element_type=jnp.float32)
    mine_x = jnp.where((lane // SUB) % 2 == 0, x[:held], x[held:])
    mine_x = jnp.concatenate([mine_x, jnp.zeros((8 - held, F), jnp.float32)], 0)

    p, q = stations[0:1, :], stations[1:2, :]
    names = jnp.concatenate([jnp.zeros((4, L), jnp.int32), p // held, p % held, q // held, q % held], 0)
    names = names.astype(jnp.float32).astype(jnp.bfloat16)

    def one(o, carry):
        own = (iota((LANES, L), 0) + o * capx == slots).astype(jnp.float32).astype(jnp.bfloat16)
        listed = lax.dot_general(names, own, (((1,), (1,)), ((), ())), preferred_element_type=jnp.float32)
        listed = jnp.concatenate([listed] + [jnp.zeros((8, F - LANES), jnp.float32)], 1)
        extras[o] = jnp.where(iota((8, F), 0) < 4, mine_x, listed).astype(jnp.bfloat16)
        return carry

    lax.fori_loop(0, B, one, 0, unroll=min(B, 8))


def index_tables(T, L, B, cap, capx, held, owners, stations, screens):
    F = SUB // T // 2 * LANES
    vmem = pl.BlockSpec(memory_space=pltpu.VMEM)
    return pl.pallas_call(
        functools.partial(index_kernel, T, L, B, cap, capx, held),
        out_shape=(
            jax.ShapeDtypeStruct((B * capx, L), jnp.bfloat16),
            jax.ShapeDtypeStruct((B, 8, F), jnp.bfloat16),
        ),
        in_specs=[vmem] * 3,
        out_specs=(vmem, vmem),
        name="index",
        cost_estimate=pl.CostEstimate(flops=10**7, bytes_accessed=10**6, transcendentals=0),
        **PARAMS,
    )(owners, stations, screens)


def send_kernel(T, L, B, cap, capx, *refs):
    terms, (hot, extras, out, rows) = refs[:-4], refs[-4:]
    Q2 = SUB // T // 2
    F = Q2 * LANES
    total = terms[0][0].astype(jnp.float32)
    for t in terms[1:]:
        total = total + t[0].astype(jnp.float32)
    rows[...] = total.reshape(L * Q2, LANES)
    for q in range(Q2):
        x = rows[pl.ds(q, L, stride=Q2), :].astype(jnp.bfloat16)
        moved = jnp.dot(hot[...], x, preferred_element_type=jnp.float32).astype(jnp.bfloat16)
        out[:, :, LANES * q : LANES * (q + 1)] = moved.reshape(B, capx, LANES)
    out[:, cap : cap + 8, :] = extras[...]


def send_blocks(T, L, B, cap, capx, terms, hot, extras):
    Q2 = SUB // T // 2
    F = Q2 * LANES
    vmem = pl.BlockSpec(memory_space=pltpu.VMEM)
    return pl.pallas_call(
        functools.partial(send_kernel, T, L, B, cap, capx),
        out_shape=jax.ShapeDtypeStruct((B, capx, F), jnp.bfloat16),
        in_specs=[vmem] * (len(terms) + 2),
        out_specs=vmem,
        scratch_shapes=[pltpu.VMEM((L * Q2, LANES), jnp.float32)],
        name="send",
        **PARAMS,
    )(*terms, hot, extras)


def rows_kernel(T, S, row_off, rows):
    Q2 = SUB // T // 2
    K = 2 * Q2 * S
    chunk, half = TILE // T, TILE // 2
    a = lax.axis_index("tm")
    index = iota((1, K), 1) // S
    m = (T * ((index % 2) * Q2 + index // 2) + a).astype(jnp.float32) * (1.0 / SUB)
    er, ei = turn(iota((SUB, K), 0).astype(jnp.float32) * m)
    for d in range(T):
        for e in range(chunk // SUB):
            r = (a ^ d) * chunk + e * SUB + iota((SUB, K), 0) - row_off[...]
            mask = (r >= 0) & (r < SUB)
            at = bit_reverse(d // 2, T // 2) * chunk + e * SUB
            rows[d % 2, at : at + SUB, :] = jnp.where(mask, er, 0.0).astype(jnp.bfloat16)
            rows[d % 2, half + at : half + at + SUB, :] = jnp.where(mask, ei, 0.0).astype(jnp.bfloat16)


def row_tables(T, S, row_off):
    K = SUB // T * S
    vmem = pl.BlockSpec(memory_space=pltpu.VMEM)
    return pl.pallas_call(
        functools.partial(rows_kernel, T, S),
        out_shape=jax.ShapeDtypeStruct((2, TILE, K), jnp.bfloat16),
        in_specs=[vmem],
        out_specs=vmem,
        name="rows",
        cost_estimate=pl.CostEstimate(flops=10**7, bytes_accessed=10**6, transcendentals=0),
        **PARAMS,
    )(row_off)


def tile_part(T, rows, spread):
    both = jnp.dot(rows, spread, preferred_element_type=jnp.float32)
    u, v = both[: TILE // 2], both[TILE // 2 :]
    tile = jnp.concatenate([u[:, :TILE] + v[:, TILE:], u[:, TILE:] - v[:, :TILE]], 1)
    return tile.reshape(T // 2, TILE // T, 2 * TILE)


def place_kernel(T, B, cap, capx, held, blocks, col_off, rows, weights, spread, send, data, gains, hot):
    Q, Q2 = SUB // T, SUB // T // 2
    F = Q2 * LANES
    S = B * cap
    NX = B * 8
    a = lax.axis_index("tm")
    lane_f = iota((8, F), 1)
    part_f = (lane_f // SUB) % 2

    def gather(b, carry):
        data[pl.ds(b * cap, cap), :] = blocks[b, 0:cap, :].astype(jnp.float32)
        x = blocks[b, cap : cap + 8, :].astype(jnp.float32)
        at = pl.ds(pl.multiple_of(b * 8, 8), 8)
        gains[at, 0:F] = jnp.where(part_f == 0, x, pltpu.roll(x, SUB, 1))
        gains[at, F : 2 * F] = jnp.where(part_f == 1, x, pltpu.roll(x, F - SUB, 1))
        same = iota((cap, LANES), 0) == iota((cap, LANES), 1)
        for k in range(2):
            number = x[4 + 2 * k : 5 + 2 * k, 0:LANES] * 8.0 + x[5 + 2 * k : 6 + 2 * k, 0:LANES]
            number = jnp.sum(jnp.where(same, jnp.broadcast_to(number, (cap, LANES)), 0.0), axis=1, keepdims=True)
            hit = number.astype(jnp.int32) == iota((cap, NX), 1)
            hot[k, pl.ds(b * cap, cap), :] = hit.astype(jnp.float32)
        return carry

    lax.fori_loop(0, B, gather, 0, unroll=min(B, 8))

    hot_p, hot_q = hot[0].astype(jnp.bfloat16), hot[1].astype(jnp.bfloat16)
    lane = iota((1, LANES), 1)
    low, l = lane // (LANES // 2), column_of(lane % SUB)
    away = [(iota((S, LANES), 1) + LANES * v) - col_off[...] for v in range(2)]
    inside = [(w >= 0) & (w < SUB) for w in away]

    def taper(n):
        scaled = (n.astype(jnp.float32) + 0.5 - SUB / 2.0) / (SUB / 2.0)
        return 1.0 - scaled * scaled

    for q in range(Q2):
        at = slice(LANES * q, LANES * (q + 1))
        at_i = slice(F + LANES * q, F + LANES * (q + 1))
        m = T * (low * Q2 + q) + a
        window = taper(m) * taper(l) * (1.0 / (SUB * 16.0))
        tables = [gains[:, at].astype(jnp.bfloat16), gains[:, at_i].astype(jnp.bfloat16)]
        pr, pi = [jnp.dot(hot_p, t, preferred_element_type=jnp.float32) for t in tables]
        qr, qi = [jnp.dot(hot_q, t, preferred_element_type=jnp.float32) for t in tables]
        d = data[:, at] * window
        x = jnp.concatenate([d * (pr * qr + pi * qi), d * (pr * qi - pi * qr)], 1).astype(jnp.bfloat16)
        y = jnp.dot(x, weights[...], preferred_element_type=jnp.float32)
        for h in range(2):
            for c in range(2):
                v = y[:, (h * 2 + c) * LANES : (h * 2 + c + 1) * LANES]
                for half in range(2):
                    spread[pl.ds((q * 2 + h) * S, S), (c * 2 + half) * LANES : (c * 2 + half + 1) * LANES] = jnp.where(
                        inside[half], v, 0.0
                    ).astype(jnp.bfloat16)

    send[...] = tile_part(T, rows[1], spread[...]).astype(jnp.bfloat16)


def place_blocks(T, B, cap, capx, held, blocks, col_off, rows, weights):
    Q2 = SUB // T // 2
    F, S, K = Q2 * LANES, B * cap, 2 * Q2 * B * cap
    vmem = pl.BlockSpec(memory_space=pltpu.VMEM)
    return pl.pallas_call(
        functools.partial(place_kernel, T, B, cap, capx, held),
        out_shape=(
            jax.ShapeDtypeStruct((K, 2 * TILE), jnp.bfloat16),
            jax.ShapeDtypeStruct((T // 2, TILE // T, 2 * TILE), jnp.bfloat16),
        ),
        in_specs=[vmem] * 4,
        out_specs=(vmem, vmem),
        scratch_shapes=[
            pltpu.VMEM((S, F), jnp.float32),
            pltpu.VMEM((B * 8, 2 * F), jnp.float32),
            pltpu.VMEM((2, S, B * 8), jnp.float32),
        ],
        name="place",
        **PARAMS,
    )(blocks, col_off, rows, weights)


def keep_kernel(T, rows, spread, keep):
    keep[...] = tile_part(T, rows[0], spread[...])


def kept_rows(T, rows, spread):
    vmem = pl.BlockSpec(memory_space=pltpu.VMEM)
    return pl.pallas_call(
        functools.partial(keep_kernel, T),
        out_shape=jax.ShapeDtypeStruct((T // 2, TILE // T, 2 * TILE), jnp.float32),
        in_specs=[vmem] * 2,
        out_specs=vmem,
        name="keep",
        cost_estimate=pl.CostEstimate(flops=10**8, bytes_accessed=10**6, transcendentals=0),
        **PARAMS,
    )(rows, spread)


def transform_weights():
    lam = np.arange(SUB)
    l = np.where(lam < SUB // 2, lam + SUB // 2, SUB - 1 - lam)
    angle = 2.0 * math.pi * (l[:, None] * (np.arange(LANES)[None, :] % SUB) % SUB) / SUB
    cos, sin = np.cos(angle), np.sin(angle)
    out = np.zeros((2, 2, 2, SUB, 2, 2, LANES))
    for h in range(2):
        out[0, h, 0, :, h, 0], out[0, h, 0, :, h, 1] = cos, -sin
        out[0, h, 1, :, h, 0], out[0, h, 1, :, h, 1] = sin, cos
        out[1, h, 1, :, h, 0], out[1, h, 1, :, h, 1] = -cos, sin
        out[1, h, 0, :, h, 0], out[1, h, 0, :, h, 1] = sin, cos
    return jnp.asarray(out.reshape(2 * LANES, 4 * LANES), jnp.float32).astype(jnp.bfloat16)


def halve(T, keep, send, late=()):
    swap = lambda x, d: lax.ppermute(x, "tm", [(i, i ^ d) for i in range(T)])
    terms, d = [keep, swap(send, 1)], 2
    while d < T:
        half = T // d // 2
        moving = sum(t[half : 2 * half].astype(jnp.float32) for t in terms).astype(jnp.bfloat16)
        if late and d == 2:
            moving, *late = lax.optimization_barrier((moving, *late))
        terms.append(swap(moving, d))
        d *= 2
    return terms, late


def per_device(visibilities, coords, counts, stations, owners, offsets, screens):
    T, B = lax.axis_size("tm"), lax.axis_size("base")
    L, slots = visibilities.shape[1], visibilities.shape[3]
    base = lax.axis_index("base")
    Q2 = SUB // T // 2
    held = screens.shape[0]
    cap = -(-max(2, 3 * L // (2 * B)) // 8) * 8
    capx = cap + 8

    def flat(x):
        return x.reshape(L, 2, slots // LANES, LANES).transpose(0, 2, 1, 3).reshape(4 * L, LANES)

    keep, send = images(T, L, counts, offsets.T, flat(coords[0]), flat(visibilities[0]))
    terms, late = halve(T, keep, send, (owners, stations, screens))
    owner = late[0][:, 0].reshape(B, L)
    hot, extras = index_tables(T, L, B, cap, capx, held, owner, late[1].T, late[2])
    outgoing = send_blocks(T, L, B, cap, capx, terms, hot, extras)
    outgoing, owners, offsets = lax.optimization_barrier((outgoing, owners, offsets))

    to_me = owners[:, 0].reshape(B, L) == base
    order = jnp.arange(L, dtype=jnp.int32)
    earlier = order[:, None] < order[None, :]
    before = jnp.sum((to_me[:, :, None] & earlier[None]).astype(jnp.int32), axis=1)
    chosen = to_me[:, None, :] & (before[:, None, :] == jnp.arange(cap, dtype=jnp.int32)[None, :, None])
    offs = offsets.T.reshape(2, B, 1, L)
    slot_offs = jnp.sum(jnp.where(chosen[None], offs, 0), axis=3).reshape(2, B * cap)
    col_off = slot_offs[1][:, None]
    row_off = jnp.tile(slot_offs[0], 2 * Q2)[None, :]

    incoming = lax.all_to_all(outgoing, "base", split_axis=0, concat_axis=0, tiled=True)
    rows = row_tables(T, B * cap, row_off)
    spread, send = place_blocks(T, B, cap, capx, held, incoming, col_off, rows, transform_weights())
    terms, _ = halve(T, kept_rows(T, rows, spread), send)
    tile = sum(t[0].astype(jnp.float32) for t in terms)
    return tile.reshape(1, TILE // T, 2, TILE)


def solution(mesh):
    return jax.shard_map(
        per_device,
        mesh=mesh,
        in_specs=(
            P("tm", "base", None, None),
            P("tm", "base", None, None),
            P("tm", "base"),
            P("base", None),
            P(),
            P(),
            P("base", None, None),
        ),
        out_specs=P("base", "tm", None, None),
        check_vma=False,
    )
```

```python
import functools
import math

import jax
import jax.numpy as jnp
import numpy as np
from jax import lax
from jax.experimental import pallas as pl
from jax.experimental.pallas import tpu as pltpu
from jax.sharding import PartitionSpec as P

SUB = 32
TILE = 256
LANES = 128
GROUP = 64
SINE = (4.442883014678955, -7.308245658874512, 3.6063544750213623, -0.8461129069328308, 0.10982698202133179)
COSINE = (1.4142135381698608, -6.978850841522217, 5.7394609451293945, -1.8835626224777222, 0.31069815158843994)
PARAMS = dict(compiler_params=pltpu.CompilerParams(vmem_limit_bytes=48 * 1024 * 1024))


def iota(shape, axis):
    return lax.broadcasted_iota(jnp.int32, shape, axis)


def turn(x):
    t = x - jnp.round(x)
    u = t * t
    s = ((((SINE[4] * u + SINE[3]) * u + SINE[2]) * u + SINE[1]) * u + SINE[0]) * t
    c = (((COSINE[4] * u + COSINE[3]) * u + COSINE[2]) * u + COSINE[1]) * u + COSINE[0]
    return 1.0 - s * s, s * c


def times(xr, xi, yr, yi):
    return xr * yr - xi * yi, xr * yi + xi * yr


def bit_reverse(i, size):
    out = 0
    while size > 1:
        out, i, size = out * 2 + i % 2, i // 2, size // 2
    return out


def column_of(lane):
    half = SUB // 2
    return jnp.where(lane < half, lane + half, SUB - 1 - lane)


def images_kernel(T, L, G, in_counts, in_offsets, in_coords, in_vis, keep, send, cs, vs, vis, counts, offsets, sems, *tables):
    Q, Q2 = SUB // T, SUB // T // 2
    half_u = SUB // 2
    a, base = lax.axis_index("tm"), lax.axis_index("base")
    parts = 2
    span = 4 * L // parts
    numbers = [
        pltpu.make_async_copy(in_counts, counts, sems.at[0]),
        pltpu.make_async_copy(in_offsets.at[:, pl.ds(pl.multiple_of(base * L, LANES), L)], offsets, sems.at[1]),
    ]
    loads = []
    for k in range(parts):
        at = pl.ds(k * span, span)
        loads.append(pltpu.make_async_copy(in_coords.at[at, :], cs.at[at, :], sems.at[2 + 2 * k]))
        loads.append(pltpu.make_async_copy(in_vis.at[at, :], vis.at[at, :], sems.at[3 + 2 * k]))
    for copy in numbers + loads:
        copy.start()

    row8, lane8 = iota((8, LANES), 0), iota((8, LANES), 1)
    owner, slot = row8 // 2, lane8 + LANES * (row8 % 2)
    low = lane8 < LANES // 2

    def pick(values):
        out = values[-1]
        for k in range(len(values) - 2, -1, -1):
            out = jnp.where(owner == k, values[k], out)
        return out

    def powers(first, n, place_c, place_v, lr, li, uc, us):
        subs = [first + 4 * n + k for k in range(4)]
        even, odd = pl.ds(16 * n, 8, stride=2), pl.ds(16 * n + 1, 8, stride=2)
        row_off, col_off = [offsets[0, k] for k in subs], [offsets[1, k] for k in subs]
        signs = [(1 - 2 * ((r + c) & 1)).astype(jnp.float32) for r, c in zip(row_off, col_off)]
        cu = place_c[even, :] + pick([(c & (SUB - 1)).astype(jnp.float32) for c in col_off])
        cv = place_c[odd, :] + pick([(r & (SUB - 1)).astype(jnp.float32) for r in row_off])
        scale = jnp.where(slot < pick([counts[0, k] for k in subs]), pick(signs), 0.0)
        vr, vi = place_v[even, :] * scale, place_v[odd, :] * scale

        half = turn(cu * (0.5 / SUB))
        step = times(*half, *half)
        e = half
        for k in range(half_u):
            uc[(n * half_u + k) * 8 : (n * half_u + k) * 8 + 8, :] = e[0]
            us[(n * half_u + k) * 8 : (n * half_u + k) * 8 + 8, :] = e[1]
            if k + 1 < half_u:
                e = times(*e, *step)
        y1 = turn(cv * (1.0 / SUB))
        y2 = times(*y1, *y1)
        y4 = times(*y2, *y2)
        w0 = times(vr, vi, *turn(cv * -0.5 - cu * (0.5 / SUB)))
        w1 = times(*w0, *y1)
        chain = [w0, w1, times(*w0, *y2), times(*w1, *y2)]
        for m in range(SUB):
            w = chain[m % 4]
            at = pl.multiple_of((n * SUB + ((m % T) ^ a) * Q + m // T) * 8, 8)
            lr[pl.ds(at, 8), :] = w[0]
            li[pl.ds(at, 8), :] = w[1]
            if m + 4 < SUB:
                chain[m % 4] = times(*w, *y4)

    def sides(n, lr, li, uc, us):
        lhs, cos_u, sin_u = [], [], []
        for ref in (lr, li):
            lhs += [ref[pl.ds((n // 4) * SUB * 8 + (2 * n + b) % 8, SUB, stride=8), :].astype(jnp.bfloat16) for b in range(2)]
        for b in range(2):
            at = pl.ds((n // 4) * half_u * 8 + (2 * n + b) % 8, half_u, stride=8)
            cos_u.append(uc[at, :].astype(jnp.bfloat16))
            sin_u.append(us[at, :].astype(jnp.bfloat16))
        neg_u = [-x for x in sin_u]
        rhs = [cos_u + neg_u, cos_u + sin_u, sin_u + cos_u, neg_u + cos_u]
        return jnp.concatenate(lhs, 1), [jnp.concatenate(r, 1) for r in rhs]

    def products(keep, send, n, *refs):
        s = 2 * n
        (l0, r0), (l1, r1) = sides(2 * n, *refs), sides(2 * n + 1, *refs)
        out = lax.dot_general(
            jnp.concatenate([l0, l1], 0),
            jnp.concatenate(r0 + r1, 0),
            (((1,), (1,)), ((), ())),
            preferred_element_type=jnp.float32,
        )
        group = max(1, 8 // Q)
        for g in range(4):
            x, y = out[8 * g : 8 * g + 8], out[SUB + 8 * g : SUB + 8 * g + 8]
            x = jnp.where(low, x, pltpu.roll(pltpu.roll(x, 8 - Q2, 0), LANES // 2, 1)).astype(jnp.bfloat16)
            y = jnp.where(low, pltpu.roll(y, LANES // 2, 1), pltpu.roll(y, 8 - Q2, 0)).astype(jnp.bfloat16)
            for k in range(group):
                d = g * group + k
                place = bit_reverse(d // 2, T // 2)
                ref = send if d % 2 else keep
                ref[place, s] = x[k * Q : k * Q + Q2]
                ref[place, s + 1] = y[k * Q : k * Q + Q2]

    for copy in numbers:
        copy.wait()
    sides_of = [tables[0:4], tables[4:8]]
    total = L // G

    def arrive(k):
        loads[2 * k].wait()
        loads[2 * k + 1].wait()
        vs[k * span : (k + 1) * span, :] = vis[k * span : (k + 1) * span, :].astype(jnp.float32)

    def make(i, side):
        at = pl.ds(pl.multiple_of(i * G * 4, 8), G * 4)
        for n in range(G // 4):
            powers(i * G, n, cs.at[at, :], vs.at[at, :], *sides_of[side])

    def use(i, side):
        at = pl.ds(i * G, G)
        for n in range(G // 2):
            products(keep.at[:, at], send.at[:, at], n, *sides_of[side])

    def step(j, carry):
        make(2 * j + 1, 1)
        use(2 * j, 0)
        make(2 * j + 2, 0)
        use(2 * j + 1, 1)
        return carry

    arrive(0)
    make(0, 0)
    for k in range(1, parts):
        arrive(k)
    lax.fori_loop(0, total // 2 - 1, step, 0)
    make(total - 1, 1)
    use(total - 2, 0)
    use(total - 1, 1)


def images(T, L, counts, offsets, coords, vis):
    Q2, G = SUB // T // 2, GROUP
    half = jax.ShapeDtypeStruct((T // 2, L, Q2, LANES), jnp.bfloat16)
    hbm, vmem = pl.BlockSpec(memory_space=pltpu.HBM), pl.BlockSpec(memory_space=pltpu.VMEM)
    table = lambda n: pltpu.VMEM((2 * G * n, LANES), jnp.float32)
    return pl.pallas_call(
        functools.partial(images_kernel, T, L, G),
        out_shape=(half, half),
        in_specs=[hbm] * 4,
        out_specs=(vmem, vmem),
        scratch_shapes=[pltpu.VMEM((4 * L, LANES), jnp.float32)] * 2
        + [
            pltpu.VMEM((4 * L, LANES), jnp.bfloat16),
            pltpu.SMEM((1, L), jnp.int32),
            pltpu.SMEM((2, L), jnp.int32),
            pltpu.SemaphoreType.DMA((6,)),
        ]
        + [table(SUB), table(SUB), table(SUB // 2), table(SUB // 2)] * 2,
        name="images",
        **PARAMS,
    )(*[pltpu.with_memory_space_constraint(x, pltpu.HBM) for x in (counts, offsets, coords, vis)])


def index_kernel(T, L, B, cap, capx, held, owners, stations, screens, first, second, hot, partial, rows):
    Q2 = SUB // T // 2
    F = Q2 * LANES
    a, base = lax.axis_index("tm"), lax.axis_index("base")
    mine = jnp.broadcast_to(owners[pl.ds(base, 1), :], (L, L))
    same = (mine == mine.T) & (iota((L, L), 0) < iota((L, L), 1))
    rank = jnp.sum(same.astype(jnp.float32), axis=0, keepdims=True).astype(jnp.int32)
    slots = mine[0:1] * capx + rank
    hot[...] = (iota((B * capx, L), 0) == slots).astype(jnp.float32).astype(jnp.bfloat16)
    for k, term in enumerate((first, second)):
        rows[k] = term[0].astype(jnp.float32).reshape(L * Q2, LANES)
    for q in range(Q2):
        parts = [rows[k, pl.ds(q, L, stride=Q2), :].astype(jnp.bfloat16) for k in range(2)]
        parts = [jnp.dot(hot[...], x, preferred_element_type=jnp.float32) for x in parts]
        partial[:, LANES * q : LANES * (q + 1)] = parts[0] + parts[1]

    lane = iota((1, F), 1)
    m = T * (((lane // (2 * SUB)) % 2) * Q2 + lane // LANES) + a
    pixel = m * SUB + column_of(lane % SUB)
    select = (iota((SUB * SUB, F), 0) == pixel).astype(jnp.float32).astype(jnp.bfloat16)
    x = jnp.concatenate([screens[:, 0, :].astype(jnp.float32), screens[:, 1, :].astype(jnp.float32)], 0)
    x = jnp.dot(x.astype(jnp.bfloat16), select, preferred_element_type=jnp.float32)
    mine_x = jnp.where((lane // SUB) % 2 == 0, x[:held], x[held:])
    mine_x = jnp.concatenate([mine_x, jnp.zeros((8 - held, F), jnp.float32)], 0)

    p, q = stations[0:1, :], stations[1:2, :]
    names = jnp.concatenate([jnp.zeros((4, L), jnp.int32), p // held, p % held, q // held, q % held], 0)
    names = names.astype(jnp.float32).astype(jnp.bfloat16)

    def one(o, carry):
        own = (iota((LANES, L), 0) + o * capx == slots).astype(jnp.float32).astype(jnp.bfloat16)
        listed = lax.dot_general(names, own, (((1,), (1,)), ((), ())), preferred_element_type=jnp.float32)
        listed = jnp.concatenate([listed] + [jnp.zeros((8, F - LANES), jnp.float32)], 1)
        at = pl.ds(pl.multiple_of(o * capx + cap, 8), 8)
        partial[at, :] = jnp.where(iota((8, F), 0) < 4, mine_x, listed)
        return carry

    lax.fori_loop(0, B, one, 0, unroll=min(B, 8))


def index_tables(T, L, B, cap, capx, held, owners, stations, screens, first, second):
    F = SUB // T // 2 * LANES
    vmem = pl.BlockSpec(memory_space=pltpu.VMEM)
    return pl.pallas_call(
        functools.partial(index_kernel, T, L, B, cap, capx, held),
        out_shape=(
            jax.ShapeDtypeStruct((B * capx, L), jnp.bfloat16),
            jax.ShapeDtypeStruct((B * capx, F), jnp.float32),
        ),
        in_specs=[vmem] * 5,
        out_specs=(vmem, vmem),
        scratch_shapes=[pltpu.VMEM((2, L * SUB // T // 2, LANES), jnp.float32)],
        name="index",
        cost_estimate=pl.CostEstimate(flops=10**7, bytes_accessed=10**6, transcendentals=0),
        **PARAMS,
    )(owners, stations, screens, first, second)


def send_kernel(T, L, B, cap, capx, *refs):
    terms, (hot, partial, out, rows, block, sems) = refs[:-6], refs[-6:]
    Q2 = SUB // T // 2
    total = terms[0][0].astype(jnp.float32)
    for t in terms[1:]:
        total = total + t[0].astype(jnp.float32)
    rows[...] = total.reshape(L * Q2, LANES)
    copies = []
    for q in range(Q2):
        at = slice(LANES * q, LANES * (q + 1))
        x = rows[pl.ds(q, L, stride=Q2), :].astype(jnp.bfloat16)
        moved = partial[:, at] + jnp.dot(hot[...], x, preferred_element_type=jnp.float32)
        block[:, :, at] = moved.astype(jnp.bfloat16).reshape(B, capx, LANES)
        copies.append(pltpu.make_async_copy(block.at[:, :, at], out.at[:, :, at], sems.at[q]))
        copies[-1].start()
    for copy in copies:
        copy.wait()


def send_blocks(T, L, B, cap, capx, terms, hot, partial):
    Q2 = SUB // T // 2
    F = Q2 * LANES
    vmem = pl.BlockSpec(memory_space=pltpu.VMEM)
    return pl.pallas_call(
        functools.partial(send_kernel, T, L, B, cap, capx),
        out_shape=jax.ShapeDtypeStruct((B, capx, F), jnp.bfloat16),
        in_specs=[vmem] * (len(terms) + 2),
        out_specs=pl.BlockSpec(memory_space=pltpu.HBM),
        scratch_shapes=[
            pltpu.VMEM((L * Q2, LANES), jnp.float32),
            pltpu.VMEM((B, capx, F), jnp.bfloat16),
            pltpu.SemaphoreType.DMA((Q2,)),
        ],
        name="send",
        **PARAMS,
    )(*terms, hot, partial)


def rows_kernel(T, S, row_off, rows):
    Q2 = SUB // T // 2
    K = 2 * Q2 * S
    chunk, half = TILE // T, TILE // 2
    a = lax.axis_index("tm")
    index = iota((1, K), 1) // S
    m = (T * ((index % 2) * Q2 + index // 2) + a).astype(jnp.float32) * (1.0 / SUB)
    er, ei = turn(iota((SUB, K), 0).astype(jnp.float32) * m)
    for d in range(T):
        for e in range(chunk // SUB):
            r = (a ^ d) * chunk + e * SUB + iota((SUB, K), 0) - row_off[...]
            mask = (r >= 0) & (r < SUB)
            at = bit_reverse(d // 2, T // 2) * chunk + e * SUB
            rows[d % 2, at : at + SUB, :] = jnp.where(mask, er, 0.0).astype(jnp.bfloat16)
            rows[d % 2, half + at : half + at + SUB, :] = jnp.where(mask, ei, 0.0).astype(jnp.bfloat16)


def row_tables(T, S, row_off):
    K = SUB // T * S
    vmem = pl.BlockSpec(memory_space=pltpu.VMEM)
    return pl.pallas_call(
        functools.partial(rows_kernel, T, S),
        out_shape=jax.ShapeDtypeStruct((2, TILE, K), jnp.bfloat16),
        in_specs=[vmem],
        out_specs=vmem,
        name="rows",
        cost_estimate=pl.CostEstimate(flops=10**7, bytes_accessed=10**6, transcendentals=0),
        **PARAMS,
    )(row_off)


def tile_part(T, rows, spread):
    both = jnp.dot(rows, spread, preferred_element_type=jnp.float32)
    u, v = both[: TILE // 2], both[TILE // 2 :]
    tile = jnp.concatenate([u[:, :TILE] + v[:, TILE:], u[:, TILE:] - v[:, :TILE]], 1)
    return tile.reshape(T // 2, TILE // T, 2 * TILE)


def place_kernel(T, B, cap, capx, held, blocks, col_off, rows, weights, spread, send, data, gains, hot):
    Q, Q2 = SUB // T, SUB // T // 2
    F = Q2 * LANES
    S = B * cap
    NX = B * 8
    a = lax.axis_index("tm")
    lane_f = iota((8, F), 1)
    part_f = (lane_f // SUB) % 2

    def gather(b, carry):
        data[pl.ds(b * cap, cap), :] = blocks[b, 0:cap, :].astype(jnp.float32)
        x = blocks[b, cap : cap + 8, :].astype(jnp.float32)
        at = pl.ds(pl.multiple_of(b * 8, 8), 8)
        gains[at, 0:F] = jnp.where(part_f == 0, x, pltpu.roll(x, SUB, 1))
        gains[at, F : 2 * F] = jnp.where(part_f == 1, x, pltpu.roll(x, F - SUB, 1))
        same = iota((cap, LANES), 0) == iota((cap, LANES), 1)
        for k in range(2):
            number = x[4 + 2 * k : 5 + 2 * k, 0:LANES] * 8.0 + x[5 + 2 * k : 6 + 2 * k, 0:LANES]
            number = jnp.sum(jnp.where(same, jnp.broadcast_to(number, (cap, LANES)), 0.0), axis=1, keepdims=True)
            hit = number.astype(jnp.int32) == iota((cap, NX), 1)
            hot[k, pl.ds(b * cap, cap), :] = hit.astype(jnp.float32)
        return carry

    lax.fori_loop(0, B, gather, 0, unroll=min(B, 8))

    hot_p, hot_q = hot[0].astype(jnp.bfloat16), hot[1].astype(jnp.bfloat16)
    lane = iota((1, LANES), 1)
    low, l = lane // (LANES // 2), column_of(lane % SUB)
    away = [(iota((S, LANES), 1) + LANES * v) - col_off[...] for v in range(2)]
    inside = [(w >= 0) & (w < SUB) for w in away]

    def taper(n):
        scaled = (n.astype(jnp.float32) + 0.5 - SUB / 2.0) / (SUB / 2.0)
        return 1.0 - scaled * scaled

    for q in range(Q2):
        at = slice(LANES * q, LANES * (q + 1))
        at_i = slice(F + LANES * q, F + LANES * (q + 1))
        m = T * (low * Q2 + q) + a
        window = taper(m) * taper(l) * (1.0 / (SUB * 16.0))
        tables = [gains[:, at].astype(jnp.bfloat16), gains[:, at_i].astype(jnp.bfloat16)]
        pr, pi = [jnp.dot(hot_p, t, preferred_element_type=jnp.float32) for t in tables]
        qr, qi = [jnp.dot(hot_q, t, preferred_element_type=jnp.float32) for t in tables]
        d = data[:, at] * window
        x = jnp.concatenate([d * (pr * qr + pi * qi), d * (pr * qi - pi * qr)], 1).astype(jnp.bfloat16)
        y = jnp.dot(x, weights[...], preferred_element_type=jnp.float32)
        for h in range(2):
            for c in range(2):
                v = y[:, (h * 2 + c) * LANES : (h * 2 + c + 1) * LANES]
                for half in range(2):
                    spread[pl.ds((q * 2 + h) * S, S), (c * 2 + half) * LANES : (c * 2 + half + 1) * LANES] = jnp.where(
                        inside[half], v, 0.0
                    ).astype(jnp.bfloat16)

    send[...] = tile_part(T, rows[1], spread[...]).astype(jnp.bfloat16)


def place_blocks(T, B, cap, capx, held, blocks, col_off, rows, weights):
    Q2 = SUB // T // 2
    F, S, K = Q2 * LANES, B * cap, 2 * Q2 * B * cap
    vmem = pl.BlockSpec(memory_space=pltpu.VMEM)
    return pl.pallas_call(
        functools.partial(place_kernel, T, B, cap, capx, held),
        out_shape=(
            jax.ShapeDtypeStruct((K, 2 * TILE), jnp.bfloat16),
            jax.ShapeDtypeStruct((T // 2, TILE // T, 2 * TILE), jnp.bfloat16),
        ),
        in_specs=[vmem] * 4,
        out_specs=(vmem, vmem),
        scratch_shapes=[
            pltpu.VMEM((S, F), jnp.float32),
            pltpu.VMEM((B * 8, 2 * F), jnp.float32),
            pltpu.VMEM((2, S, B * 8), jnp.float32),
        ],
        name="place",
        **PARAMS,
    )(blocks, col_off, rows, weights)


def keep_kernel(T, rows, spread, keep):
    keep[...] = tile_part(T, rows[0], spread[...])


def kept_rows(T, rows, spread):
    vmem = pl.BlockSpec(memory_space=pltpu.VMEM)
    return pl.pallas_call(
        functools.partial(keep_kernel, T),
        out_shape=jax.ShapeDtypeStruct((T // 2, TILE // T, 2 * TILE), jnp.float32),
        in_specs=[vmem] * 2,
        out_specs=vmem,
        name="keep",
        cost_estimate=pl.CostEstimate(flops=10**8, bytes_accessed=10**6, transcendentals=0),
        **PARAMS,
    )(rows, spread)


def transform_weights():
    lam = np.arange(SUB)
    l = np.where(lam < SUB // 2, lam + SUB // 2, SUB - 1 - lam)
    angle = 2.0 * math.pi * (l[:, None] * (np.arange(LANES)[None, :] % SUB) % SUB) / SUB
    cos, sin = np.cos(angle), np.sin(angle)
    out = np.zeros((2, 2, 2, SUB, 2, 2, LANES))
    for h in range(2):
        out[0, h, 0, :, h, 0], out[0, h, 0, :, h, 1] = cos, -sin
        out[0, h, 1, :, h, 0], out[0, h, 1, :, h, 1] = sin, cos
        out[1, h, 1, :, h, 0], out[1, h, 1, :, h, 1] = -cos, sin
        out[1, h, 0, :, h, 0], out[1, h, 0, :, h, 1] = sin, cos
    return jnp.asarray(out.reshape(2 * LANES, 4 * LANES), jnp.float32).astype(jnp.bfloat16)


def halve(T, keep, send, late=()):
    swap = lambda x, d: lax.ppermute(x, "tm", [(i, i ^ d) for i in range(T)])
    terms, d = [keep, swap(send, 1)], 2
    while d < T:
        half = T // d // 2
        moving = sum(t[half : 2 * half].astype(jnp.float32) for t in terms).astype(jnp.bfloat16)
        if late and d == 2:
            moving, *late = lax.optimization_barrier((moving, *late))
        terms.append(swap(moving, d))
        d *= 2
    return terms, late


def per_device(visibilities, coords, counts, stations, owners, offsets, screens):
    T, B = lax.axis_size("tm"), lax.axis_size("base")
    L, slots = visibilities.shape[1], visibilities.shape[3]
    base = lax.axis_index("base")
    Q2 = SUB // T // 2
    held = screens.shape[0]
    cap = -(-max(2, 3 * L // (2 * B)) // 8) * 8
    capx = cap + 8

    def flat(x):
        return x.reshape(L, 2, slots // LANES, LANES).transpose(0, 2, 1, 3).reshape(4 * L, LANES)

    keep, send = images(T, L, counts, offsets.T, flat(coords[0]), flat(visibilities[0]))
    terms, late = halve(T, keep, send, (owners, stations, screens))
    owner = late[0][:, 0].reshape(B, L)
    hot, partial = index_tables(T, L, B, cap, capx, held, owner, late[1].T, late[2], *terms[:2])
    outgoing = send_blocks(T, L, B, cap, capx, terms[2:], hot, partial)
    outgoing, owners, offsets = lax.optimization_barrier((outgoing, owners, offsets))

    to_me = owners[:, 0].reshape(B, L) == base
    order = jnp.arange(L, dtype=jnp.int32)
    earlier = order[:, None] < order[None, :]
    before = jnp.sum((to_me[:, :, None] & earlier[None]).astype(jnp.int32), axis=1)
    chosen = to_me[:, None, :] & (before[:, None, :] == jnp.arange(cap, dtype=jnp.int32)[None, :, None])
    offs = offsets.T.reshape(2, B, 1, L)
    slot_offs = jnp.sum(jnp.where(chosen[None], offs, 0), axis=3).reshape(2, B * cap)
    col_off = slot_offs[1][:, None]
    row_off = jnp.tile(slot_offs[0], 2 * Q2)[None, :]

    incoming = lax.all_to_all(outgoing, "base", split_axis=0, concat_axis=0, tiled=True)
    rows = row_tables(T, B * cap, row_off)
    spread, send = place_blocks(T, B, cap, capx, held, incoming, col_off, rows, transform_weights())
    terms, _ = halve(T, kept_rows(T, rows, spread), send)
    tile = sum(t[0].astype(jnp.float32) for t in terms)
    return tile.reshape(1, TILE // T, 2, TILE)


def solution(mesh):
    return jax.shard_map(
        per_device,
        mesh=mesh,
        in_specs=(
            P("tm", "base", None, None),
            P("tm", "base", None, None),
            P("tm", "base"),
            P("base", None),
            P(),
            P(),
            P("base", None, None),
        ),
        out_specs=P("base", "tm", None, None),
        check_vma=False,
    )
```

```python
import functools
import math

import jax
import jax.numpy as jnp
import numpy as np
from jax import lax
from jax.experimental import pallas as pl
from jax.experimental.pallas import tpu as pltpu
from jax.sharding import PartitionSpec as P

SUB = 32
TILE = 256
LANES = 128
GROUP = 64
SINE = (4.442883014678955, -7.308245658874512, 3.6063544750213623, -0.8461129069328308, 0.10982698202133179)
COSINE = (1.4142135381698608, -6.978850841522217, 5.7394609451293945, -1.8835626224777222, 0.31069815158843994)
PARAMS = dict(compiler_params=pltpu.CompilerParams(vmem_limit_bytes=48 * 1024 * 1024))


def iota(shape, axis):
    return lax.broadcasted_iota(jnp.int32, shape, axis)


def turn(x):
    t = x - jnp.round(x)
    u = t * t
    s = ((((SINE[4] * u + SINE[3]) * u + SINE[2]) * u + SINE[1]) * u + SINE[0]) * t
    c = (((COSINE[4] * u + COSINE[3]) * u + COSINE[2]) * u + COSINE[1]) * u + COSINE[0]
    return 1.0 - s * s, s * c


def times(xr, xi, yr, yi):
    return xr * yr - xi * yi, xr * yi + xi * yr


def bit_reverse(i, size):
    out = 0
    while size > 1:
        out, i, size = out * 2 + i % 2, i // 2, size // 2
    return out


def column_of(lane):
    half = SUB // 2
    return jnp.where(lane < half, lane + half, SUB - 1 - lane)


def images_kernel(T, L, G, in_counts, in_offsets, in_coords, in_vis, keep, send, cs, vs, vis, counts, offsets, sems, *tables):
    Q, Q2 = SUB // T, SUB // T // 2
    half_u = SUB // 2
    a, base = lax.axis_index("tm"), lax.axis_index("base")
    parts = 2
    span = 4 * L // parts
    numbers = [
        pltpu.make_async_copy(in_counts, counts, sems.at[0]),
        pltpu.make_async_copy(in_offsets.at[:, pl.ds(pl.multiple_of(base * L, LANES), L)], offsets, sems.at[1]),
    ]
    loads = []
    for k in range(parts):
        at = pl.ds(k * span, span)
        loads.append(pltpu.make_async_copy(in_coords.at[at, :], cs.at[at, :], sems.at[2 + 2 * k]))
        loads.append(pltpu.make_async_copy(in_vis.at[at, :], vis.at[at, :], sems.at[3 + 2 * k]))
    for copy in numbers + loads:
        copy.start()

    row8, lane8 = iota((8, LANES), 0), iota((8, LANES), 1)
    owner, slot = row8 // 2, lane8 + LANES * (row8 % 2)
    low = lane8 < LANES // 2

    def pick(values):
        out = values[-1]
        for k in range(len(values) - 2, -1, -1):
            out = jnp.where(owner == k, values[k], out)
        return out

    def powers(first, n, place_c, place_v, lr, li, uc, us):
        subs = [first + 4 * n + k for k in range(4)]
        even, odd = pl.ds(16 * n, 8, stride=2), pl.ds(16 * n + 1, 8, stride=2)
        row_off, col_off = [offsets[0, k] for k in subs], [offsets[1, k] for k in subs]
        signs = [(1 - 2 * ((r + c) & 1)).astype(jnp.float32) for r, c in zip(row_off, col_off)]
        cu = place_c[even, :] + pick([(c & (SUB - 1)).astype(jnp.float32) for c in col_off])
        cv = place_c[odd, :] + pick([(r & (SUB - 1)).astype(jnp.float32) for r in row_off])
        scale = jnp.where(slot < pick([counts[0, k] for k in subs]), pick(signs), 0.0)
        vr, vi = place_v[even, :] * scale, place_v[odd, :] * scale

        half = turn(cu * (0.5 / SUB))
        step = times(*half, *half)
        e = half
        for k in range(half_u):
            uc[(n * half_u + k) * 8 : (n * half_u + k) * 8 + 8, :] = e[0]
            us[(n * half_u + k) * 8 : (n * half_u + k) * 8 + 8, :] = e[1]
            if k + 1 < half_u:
                e = times(*e, *step)
        y1 = turn(cv * (1.0 / SUB))
        y2 = times(*y1, *y1)
        y4 = times(*y2, *y2)
        w0 = times(vr, vi, *turn(cv * -0.5 - cu * (0.5 / SUB)))
        w1 = times(*w0, *y1)
        chain = [w0, w1, times(*w0, *y2), times(*w1, *y2)]
        for m in range(SUB):
            w = chain[m % 4]
            at = pl.multiple_of((n * SUB + ((m % T) ^ a) * Q + m // T) * 8, 8)
            lr[pl.ds(at, 8), :] = w[0]
            li[pl.ds(at, 8), :] = w[1]
            if m + 4 < SUB:
                chain[m % 4] = times(*w, *y4)

    def sides(n, lr, li, uc, us):
        lhs, cos_u, sin_u = [], [], []
        for ref in (lr, li):
            lhs += [ref[pl.ds((n // 4) * SUB * 8 + (2 * n + b) % 8, SUB, stride=8), :].astype(jnp.bfloat16) for b in range(2)]
        for b in range(2):
            at = pl.ds((n // 4) * half_u * 8 + (2 * n + b) % 8, half_u, stride=8)
            cos_u.append(uc[at, :].astype(jnp.bfloat16))
            sin_u.append(us[at, :].astype(jnp.bfloat16))
        neg_u = [-x for x in sin_u]
        rhs = [cos_u + neg_u, cos_u + sin_u, sin_u + cos_u, neg_u + cos_u]
        return jnp.concatenate(lhs, 1), [jnp.concatenate(r, 1) for r in rhs]

    def products(keep, send, n, *refs):
        s = 2 * n
        (l0, r0), (l1, r1) = sides(2 * n, *refs), sides(2 * n + 1, *refs)
        out = lax.dot_general(
            jnp.concatenate([l0, l1], 0),
            jnp.concatenate(r0 + r1, 0),
            (((1,), (1,)), ((), ())),
            preferred_element_type=jnp.float32,
        )
        group = max(1, 8 // Q)
        for g in range(4):
            x, y = out[8 * g : 8 * g + 8], out[SUB + 8 * g : SUB + 8 * g + 8]
            x = jnp.where(low, x, pltpu.roll(pltpu.roll(x, 8 - Q2, 0), LANES // 2, 1)).astype(jnp.bfloat16)
            y = jnp.where(low, pltpu.roll(y, LANES // 2, 1), pltpu.roll(y, 8 - Q2, 0)).astype(jnp.bfloat16)
            for k in range(group):
                d = g * group + k
                place = bit_reverse(d // 2, T // 2)
                ref = send if d % 2 else keep
                ref[place, s] = x[k * Q : k * Q + Q2]
                ref[place, s + 1] = y[k * Q : k * Q + Q2]

    for copy in numbers:
        copy.wait()
    sides_of = [tables[0:4], tables[4:8]]
    total = L // G

    def arrive(k):
        loads[2 * k].wait()
        loads[2 * k + 1].wait()
        vs[k * span : (k + 1) * span, :] = vis[k * span : (k + 1) * span, :].astype(jnp.float32)

    def make(i, side):
        at = pl.ds(pl.multiple_of(i * G * 4, 8), G * 4)
        for n in range(G // 4):
            powers(i * G, n, cs.at[at, :], vs.at[at, :], *sides_of[side])

    def use(i, side):
        at = pl.ds(i * G, G)
        for n in range(G // 2):
            products(keep.at[:, at], send.at[:, at], n, *sides_of[side])

    def step(j, carry):
        make(2 * j + 1, 1)
        use(2 * j, 0)
        make(2 * j + 2, 0)
        use(2 * j + 1, 1)
        return carry

    arrive(0)
    make(0, 0)
    for k in range(1, parts):
        arrive(k)
    lax.fori_loop(0, total // 2 - 1, step, 0)
    make(total - 1, 1)
    use(total - 2, 0)
    use(total - 1, 1)


def images(T, L, counts, offsets, coords, vis):
    Q2, G = SUB // T // 2, GROUP
    half = jax.ShapeDtypeStruct((T // 2, L, Q2, LANES), jnp.bfloat16)
    hbm, vmem = pl.BlockSpec(memory_space=pltpu.HBM), pl.BlockSpec(memory_space=pltpu.VMEM)
    table = lambda n: pltpu.VMEM((2 * G * n, LANES), jnp.float32)
    return pl.pallas_call(
        functools.partial(images_kernel, T, L, G),
        out_shape=(half, half),
        in_specs=[hbm] * 4,
        out_specs=(vmem, vmem),
        scratch_shapes=[pltpu.VMEM((4 * L, LANES), jnp.float32)] * 2
        + [
            pltpu.VMEM((4 * L, LANES), jnp.bfloat16),
            pltpu.SMEM((1, L), jnp.int32),
            pltpu.SMEM((2, L), jnp.int32),
            pltpu.SemaphoreType.DMA((6,)),
        ]
        + [table(SUB), table(SUB), table(SUB // 2), table(SUB // 2)] * 2,
        name="images",
        **PARAMS,
    )(*[pltpu.with_memory_space_constraint(x, pltpu.HBM) for x in (counts, offsets, coords, vis)])


def index_kernel(T, L, B, cap, capx, held, owners, stations, screens, first, second, hot, partial, rows):
    Q2 = SUB // T // 2
    F = Q2 * LANES
    a, base = lax.axis_index("tm"), lax.axis_index("base")
    mine = jnp.broadcast_to(owners[pl.ds(base, 1), :], (L, L))
    same = (mine == mine.T) & (iota((L, L), 0) < iota((L, L), 1))
    rank = jnp.sum(same.astype(jnp.float32), axis=0, keepdims=True).astype(jnp.int32)
    slots = mine[0:1] * capx + rank
    hot[...] = (iota((B * capx, L), 0) == slots).astype(jnp.float32).astype(jnp.bfloat16)
    for k, term in enumerate((first, second)):
        rows[k] = term[0].astype(jnp.float32).reshape(L * Q2, LANES)
    for q in range(Q2):
        parts = [rows[k, pl.ds(q, L, stride=Q2), :].astype(jnp.bfloat16) for k in range(2)]
        parts = [jnp.dot(hot[...], x, preferred_element_type=jnp.float32) for x in parts]
        partial[:, LANES * q : LANES * (q + 1)] = parts[0] + parts[1]

    lane = iota((1, F), 1)
    m = T * (((lane // (2 * SUB)) % 2) * Q2 + lane // LANES) + a
    pixel = m * SUB + column_of(lane % SUB)
    select = (iota((SUB * SUB, F), 0) == pixel).astype(jnp.float32).astype(jnp.bfloat16)
    x = jnp.concatenate([screens[:, 0, :].astype(jnp.float32), screens[:, 1, :].astype(jnp.float32)], 0)
    x = jnp.dot(x.astype(jnp.bfloat16), select, preferred_element_type=jnp.float32)
    mine_x = jnp.where((lane // SUB) % 2 == 0, x[:held], x[held:])
    mine_x = jnp.concatenate([mine_x, jnp.zeros((8 - held, F), jnp.float32)], 0)

    p, q = stations[0:1, :], stations[1:2, :]
    names = jnp.concatenate([jnp.zeros((4, L), jnp.int32), p // held, p % held, q // held, q % held], 0)
    names = names.astype(jnp.float32).astype(jnp.bfloat16)

    def one(o, carry):
        own = (iota((LANES, L), 0) + o * capx == slots).astype(jnp.float32).astype(jnp.bfloat16)
        listed = lax.dot_general(names, own, (((1,), (1,)), ((), ())), preferred_element_type=jnp.float32)
        listed = jnp.concatenate([listed] + [jnp.zeros((8, F - LANES), jnp.float32)], 1)
        at = pl.ds(pl.multiple_of(o * capx + cap, 8), 8)
        partial[at, :] = jnp.where(iota((8, F), 0) < 4, mine_x, listed)
        return carry

    lax.fori_loop(0, B, one, 0, unroll=min(B, 8))


def index_tables(T, L, B, cap, capx, held, owners, stations, screens, first, second):
    F = SUB // T // 2 * LANES
    vmem = pl.BlockSpec(memory_space=pltpu.VMEM)
    return pl.pallas_call(
        functools.partial(index_kernel, T, L, B, cap, capx, held),
        out_shape=(
            jax.ShapeDtypeStruct((B * capx, L), jnp.bfloat16),
            jax.ShapeDtypeStruct((B * capx, F), jnp.float32),
        ),
        in_specs=[vmem] * 5,
        out_specs=(vmem, vmem),
        scratch_shapes=[pltpu.VMEM((2, L * SUB // T // 2, LANES), jnp.float32)],
        name="index",
        cost_estimate=pl.CostEstimate(flops=10**7, bytes_accessed=10**6, transcendentals=0),
        **PARAMS,
    )(owners, stations, screens, first, second)


def send_kernel(T, L, B, cap, capx, *refs):
    terms, (hot, partial, out, rows, block, sems) = refs[:-6], refs[-6:]
    Q2 = SUB // T // 2
    total = terms[0][0].astype(jnp.float32)
    for t in terms[1:]:
        total = total + t[0].astype(jnp.float32)
    rows[...] = total.reshape(L * Q2, LANES)
    copies = []
    for q in range(Q2):
        at = slice(LANES * q, LANES * (q + 1))
        x = rows[pl.ds(q, L, stride=Q2), :].astype(jnp.bfloat16)
        moved = partial[:, at] + jnp.dot(hot[...], x, preferred_element_type=jnp.float32)
        block[:, :, at] = moved.astype(jnp.bfloat16).reshape(B, capx, LANES)
        copies.append(pltpu.make_async_copy(block.at[:, :, at], out.at[:, :, at], sems.at[q]))
        copies[-1].start()
    for copy in copies:
        copy.wait()


def send_blocks(T, L, B, cap, capx, terms, hot, partial):
    Q2 = SUB // T // 2
    F = Q2 * LANES
    vmem = pl.BlockSpec(memory_space=pltpu.VMEM)
    return pl.pallas_call(
        functools.partial(send_kernel, T, L, B, cap, capx),
        out_shape=jax.ShapeDtypeStruct((B, capx, F), jnp.bfloat16),
        in_specs=[vmem] * (len(terms) + 2),
        out_specs=pl.BlockSpec(memory_space=pltpu.HBM),
        scratch_shapes=[
            pltpu.VMEM((L * Q2, LANES), jnp.float32),
            pltpu.VMEM((B, capx, F), jnp.bfloat16),
            pltpu.SemaphoreType.DMA((Q2,)),
        ],
        name="send",
        **PARAMS,
    )(*terms, hot, partial)


def rows_kernel(T, S, row_off, rows):
    Q2 = SUB // T // 2
    K = 2 * Q2 * S
    chunk, half = TILE // T, TILE // 2
    a = lax.axis_index("tm")
    index = iota((1, K), 1) // S
    m = (T * ((index % 2) * Q2 + index // 2) + a).astype(jnp.float32) * (1.0 / SUB)
    er, ei = turn(iota((SUB, K), 0).astype(jnp.float32) * m)
    for d in range(T):
        for e in range(chunk // SUB):
            r = (a ^ d) * chunk + e * SUB + iota((SUB, K), 0) - row_off[...]
            mask = (r >= 0) & (r < SUB)
            at = bit_reverse(d // 2, T // 2) * chunk + e * SUB
            rows[d % 2, at : at + SUB, :] = jnp.where(mask, er, 0.0).astype(jnp.bfloat16)
            rows[d % 2, half + at : half + at + SUB, :] = jnp.where(mask, ei, 0.0).astype(jnp.bfloat16)


def row_tables(T, S, row_off):
    K = SUB // T * S
    vmem = pl.BlockSpec(memory_space=pltpu.VMEM)
    return pl.pallas_call(
        functools.partial(rows_kernel, T, S),
        out_shape=jax.ShapeDtypeStruct((2, TILE, K), jnp.bfloat16),
        in_specs=[vmem],
        out_specs=vmem,
        name="rows",
        cost_estimate=pl.CostEstimate(flops=10**7, bytes_accessed=10**6, transcendentals=0),
        **PARAMS,
    )(row_off)


def tile_part(T, rows, spread):
    both = jnp.dot(rows, spread, preferred_element_type=jnp.float32)
    u, v = both[: TILE // 2], both[TILE // 2 :]
    tile = jnp.concatenate([u[:, :TILE] + v[:, TILE:], u[:, TILE:] - v[:, :TILE]], 1)
    return tile.reshape(T // 2, TILE // T, 2 * TILE)


def place_kernel(T, B, cap, capx, held, blocks, col_off, rows, weights, spread, send, data, gains, hot):
    Q, Q2 = SUB // T, SUB // T // 2
    F = Q2 * LANES
    S = B * cap
    NX = B * 8
    a = lax.axis_index("tm")
    lane_f = iota((8, F), 1)
    part_f = (lane_f // SUB) % 2

    def gather(b, carry):
        data[pl.ds(b * cap, cap), :] = blocks[b, 0:cap, :].astype(jnp.float32)
        x = blocks[b, cap : cap + 8, :].astype(jnp.float32)
        at = pl.ds(pl.multiple_of(b * 8, 8), 8)
        gains[at, 0:F] = jnp.where(part_f == 0, x, pltpu.roll(x, SUB, 1))
        gains[at, F : 2 * F] = jnp.where(part_f == 1, x, pltpu.roll(x, F - SUB, 1))
        same = iota((cap, LANES), 0) == iota((cap, LANES), 1)
        for k in range(2):
            number = x[4 + 2 * k : 5 + 2 * k, 0:LANES] * 8.0 + x[5 + 2 * k : 6 + 2 * k, 0:LANES]
            number = jnp.sum(jnp.where(same, jnp.broadcast_to(number, (cap, LANES)), 0.0), axis=1, keepdims=True)
            hit = number.astype(jnp.int32) == iota((cap, NX), 1)
            hot[k, pl.ds(b * cap, cap), :] = hit.astype(jnp.float32)
        return carry

    lax.fori_loop(0, B, gather, 0, unroll=min(B, 8))

    hot_p, hot_q = hot[0].astype(jnp.bfloat16), hot[1].astype(jnp.bfloat16)
    lane = iota((1, LANES), 1)
    low, l = lane // (LANES // 2), column_of(lane % SUB)
    away = [(iota((S, LANES), 1) + LANES * v) - col_off[...] for v in range(2)]
    inside = [(w >= 0) & (w < SUB) for w in away]

    def taper(n):
        scaled = (n.astype(jnp.float32) + 0.5 - SUB / 2.0) / (SUB / 2.0)
        return 1.0 - scaled * scaled

    mixed = []
    for q in range(Q2):
        at = slice(LANES * q, LANES * (q + 1))
        at_i = slice(F + LANES * q, F + LANES * (q + 1))
        m = T * (low * Q2 + q) + a
        window = taper(m) * taper(l) * (1.0 / (SUB * 16.0))
        tables = [gains[:, at].astype(jnp.bfloat16), gains[:, at_i].astype(jnp.bfloat16)]
        pr, pi = [jnp.dot(hot_p, t, preferred_element_type=jnp.float32) for t in tables]
        qr, qi = [jnp.dot(hot_q, t, preferred_element_type=jnp.float32) for t in tables]
        d = data[:, at] * window
        x = jnp.concatenate([d * (pr * qr + pi * qi), d * (pr * qi - pi * qr)], 1).astype(jnp.bfloat16)
        mixed.append(x)

    for q in range(Q2):
        y = jnp.dot(mixed[q], weights[...], preferred_element_type=jnp.float32)
        for h in range(2):
            for c in range(2):
                v = y[:, (h * 2 + c) * LANES : (h * 2 + c + 1) * LANES]
                for half in range(2):
                    spread[pl.ds((q * 2 + h) * S, S), (c * 2 + half) * LANES : (c * 2 + half + 1) * LANES] = jnp.where(
                        inside[half], v, 0.0
                    ).astype(jnp.bfloat16)

    send[...] = tile_part(T, rows[1], spread[...]).astype(jnp.bfloat16)


def place_blocks(T, B, cap, capx, held, blocks, col_off, rows, weights):
    Q2 = SUB // T // 2
    F, S, K = Q2 * LANES, B * cap, 2 * Q2 * B * cap
    vmem = pl.BlockSpec(memory_space=pltpu.VMEM)
    return pl.pallas_call(
        functools.partial(place_kernel, T, B, cap, capx, held),
        out_shape=(
            jax.ShapeDtypeStruct((K, 2 * TILE), jnp.bfloat16),
            jax.ShapeDtypeStruct((T // 2, TILE // T, 2 * TILE), jnp.bfloat16),
        ),
        in_specs=[vmem] * 4,
        out_specs=(vmem, vmem),
        scratch_shapes=[
            pltpu.VMEM((S, F), jnp.float32),
            pltpu.VMEM((B * 8, 2 * F), jnp.float32),
            pltpu.VMEM((2, S, B * 8), jnp.float32),
        ],
        name="place",
        **PARAMS,
    )(blocks, col_off, rows, weights)


def keep_kernel(T, rows, spread, keep):
    keep[...] = tile_part(T, rows[0], spread[...])


def kept_rows(T, rows, spread):
    vmem = pl.BlockSpec(memory_space=pltpu.VMEM)
    return pl.pallas_call(
        functools.partial(keep_kernel, T),
        out_shape=jax.ShapeDtypeStruct((T // 2, TILE // T, 2 * TILE), jnp.float32),
        in_specs=[vmem] * 2,
        out_specs=vmem,
        name="keep",
        cost_estimate=pl.CostEstimate(flops=10**8, bytes_accessed=10**6, transcendentals=0),
        **PARAMS,
    )(rows, spread)


def transform_weights():
    lam = np.arange(SUB)
    l = np.where(lam < SUB // 2, lam + SUB // 2, SUB - 1 - lam)
    angle = 2.0 * math.pi * (l[:, None] * (np.arange(LANES)[None, :] % SUB) % SUB) / SUB
    cos, sin = np.cos(angle), np.sin(angle)
    out = np.zeros((2, 2, 2, SUB, 2, 2, LANES))
    for h in range(2):
        out[0, h, 0, :, h, 0], out[0, h, 0, :, h, 1] = cos, -sin
        out[0, h, 1, :, h, 0], out[0, h, 1, :, h, 1] = sin, cos
        out[1, h, 1, :, h, 0], out[1, h, 1, :, h, 1] = -cos, sin
        out[1, h, 0, :, h, 0], out[1, h, 0, :, h, 1] = sin, cos
    return jnp.asarray(out.reshape(2 * LANES, 4 * LANES), jnp.float32).astype(jnp.bfloat16)


def halve(T, keep, send, late=()):
    swap = lambda x, d: lax.ppermute(x, "tm", [(i, i ^ d) for i in range(T)])
    terms, d = [keep, swap(send, 1)], 2
    while d < T:
        half = T // d // 2
        moving = sum(t[half : 2 * half].astype(jnp.float32) for t in terms).astype(jnp.bfloat16)
        if late and d == 2:
            moving, *late = lax.optimization_barrier((moving, *late))
        terms.append(swap(moving, d))
        d *= 2
    return terms, late


def per_device(visibilities, coords, counts, stations, owners, offsets, screens):
    T, B = lax.axis_size("tm"), lax.axis_size("base")
    L, slots = visibilities.shape[1], visibilities.shape[3]
    base = lax.axis_index("base")
    Q2 = SUB // T // 2
    held = screens.shape[0]
    cap = -(-max(2, 3 * L // (2 * B)) // 8) * 8
    capx = cap + 8

    def flat(x):
        return x.reshape(L, 2, slots // LANES, LANES).transpose(0, 2, 1, 3).reshape(4 * L, LANES)

    keep, send = images(T, L, counts, offsets.T, flat(coords[0]), flat(visibilities[0]))
    terms, late = halve(T, keep, send, (owners, stations, screens))
    owner = late[0][:, 0].reshape(B, L)
    hot, partial = index_tables(T, L, B, cap, capx, held, owner, late[1].T, late[2], *terms[:2])
    outgoing = send_blocks(T, L, B, cap, capx, terms[2:], hot, partial)
    outgoing, owners, offsets = lax.optimization_barrier((outgoing, owners, offsets))

    to_me = owners[:, 0].reshape(B, L) == base
    order = jnp.arange(L, dtype=jnp.int32)
    earlier = order[:, None] < order[None, :]
    before = jnp.sum((to_me[:, :, None] & earlier[None]).astype(jnp.int32), axis=1)
    chosen = to_me[:, None, :] & (before[:, None, :] == jnp.arange(cap, dtype=jnp.int32)[None, :, None])
    offs = offsets.T.reshape(2, B, 1, L)
    slot_offs = jnp.sum(jnp.where(chosen[None], offs, 0), axis=3).reshape(2, B * cap)
    col_off = slot_offs[1][:, None]
    row_off = jnp.tile(slot_offs[0], 2 * Q2)[None, :]

    incoming = lax.all_to_all(outgoing, "base", split_axis=0, concat_axis=0, tiled=True)
    rows = row_tables(T, B * cap, row_off)
    spread, send = place_blocks(T, B, cap, capx, held, incoming, col_off, rows, transform_weights())
    terms, _ = halve(T, kept_rows(T, rows, spread), send)
    tile = sum(t[0].astype(jnp.float32) for t in terms)
    return tile.reshape(1, TILE // T, 2, TILE)


def solution(mesh):
    return jax.shard_map(
        per_device,
        mesh=mesh,
        in_specs=(
            P("tm", "base", None, None),
            P("tm", "base", None, None),
            P("tm", "base"),
            P("base", None),
            P(),
            P(),
            P("base", None, None),
        ),
        out_specs=P("base", "tm", None, None),
        check_vma=False,
    )
```

```python
import functools
import math

import jax
import jax.numpy as jnp
import numpy as np
from jax import lax
from jax.experimental import pallas as pl
from jax.experimental.pallas import tpu as pltpu
from jax.sharding import PartitionSpec as P

SUB = 32
TILE = 256
LANES = 128
GROUP = 64
SINE = (4.442883014678955, -7.308245658874512, 3.6063544750213623, -0.8461129069328308, 0.10982698202133179)
COSINE = (1.4142135381698608, -6.978850841522217, 5.7394609451293945, -1.8835626224777222, 0.31069815158843994)
PARAMS = dict(compiler_params=pltpu.CompilerParams(vmem_limit_bytes=48 * 1024 * 1024))


def iota(shape, axis):
    return lax.broadcasted_iota(jnp.int32, shape, axis)


def turn(x):
    t = x - jnp.round(x)
    u = t * t
    s = ((((SINE[4] * u + SINE[3]) * u + SINE[2]) * u + SINE[1]) * u + SINE[0]) * t
    c = (((COSINE[4] * u + COSINE[3]) * u + COSINE[2]) * u + COSINE[1]) * u + COSINE[0]
    return 1.0 - s * s, s * c


def times(xr, xi, yr, yi):
    return xr * yr - xi * yi, xr * yi + xi * yr


def bit_reverse(i, size):
    out = 0
    while size > 1:
        out, i, size = out * 2 + i % 2, i // 2, size // 2
    return out


def column_of(lane):
    half = SUB // 2
    return jnp.where(lane < half, lane + half, SUB - 1 - lane)


def images_kernel(T, L, G, in_counts, in_offsets, in_coords, in_vis, keep, send, cs, vs, vis, counts, offsets, sems, *tables):
    Q, Q2 = SUB // T, SUB // T // 2
    half_u = SUB // 2
    a, base = lax.axis_index("tm"), lax.axis_index("base")
    parts = 2
    span = 4 * L // parts
    numbers = [
        pltpu.make_async_copy(in_counts, counts, sems.at[0]),
        pltpu.make_async_copy(in_offsets.at[:, pl.ds(pl.multiple_of(base * L, LANES), L)], offsets, sems.at[1]),
    ]
    loads = []
    for k in range(parts):
        at = pl.ds(k * span, span)
        loads.append(pltpu.make_async_copy(in_coords.at[at, :], cs.at[at, :], sems.at[2 + 2 * k]))
        loads.append(pltpu.make_async_copy(in_vis.at[at, :], vis.at[at, :], sems.at[3 + 2 * k]))
    for copy in numbers + loads:
        copy.start()

    row8, lane8 = iota((8, LANES), 0), iota((8, LANES), 1)
    owner, slot = row8 // 2, lane8 + LANES * (row8 % 2)
    low = lane8 < LANES // 2

    def pick(values):
        out = values[-1]
        for k in range(len(values) - 2, -1, -1):
            out = jnp.where(owner == k, values[k], out)
        return out

    def powers(first, n, place_c, place_v, lr, li, uc, us):
        subs = [first + 4 * n + k for k in range(4)]
        even, odd = pl.ds(16 * n, 8, stride=2), pl.ds(16 * n + 1, 8, stride=2)
        row_off, col_off = [offsets[0, k] for k in subs], [offsets[1, k] for k in subs]
        signs = [(1 - 2 * ((r + c) & 1)).astype(jnp.float32) for r, c in zip(row_off, col_off)]
        cu = place_c[even, :] + pick([(c & (SUB - 1)).astype(jnp.float32) for c in col_off])
        cv = place_c[odd, :] + pick([(r & (SUB - 1)).astype(jnp.float32) for r in row_off])
        scale = jnp.where(slot < pick([counts[0, k] for k in subs]), pick(signs), 0.0)
        vr, vi = place_v[even, :] * scale, place_v[odd, :] * scale

        half = turn(cu * (0.5 / SUB))
        step = times(*half, *half)
        e = half
        for k in range(half_u):
            uc[(n * half_u + k) * 8 : (n * half_u + k) * 8 + 8, :] = e[0]
            us[(n * half_u + k) * 8 : (n * half_u + k) * 8 + 8, :] = e[1]
            if k + 1 < half_u:
                e = times(*e, *step)
        y1 = turn(cv * (1.0 / SUB))
        y2 = times(*y1, *y1)
        y4 = times(*y2, *y2)
        w0 = times(vr, vi, *turn(cv * -0.5 - cu * (0.5 / SUB)))
        w1 = times(*w0, *y1)
        chain = [w0, w1, times(*w0, *y2), times(*w1, *y2)]
        for m in range(SUB):
            w = chain[m % 4]
            at = pl.multiple_of((n * SUB + ((m % T) ^ a) * Q + m // T) * 8, 8)
            lr[pl.ds(at, 8), :] = w[0]
            li[pl.ds(at, 8), :] = w[1]
            if m + 4 < SUB:
                chain[m % 4] = times(*w, *y4)

    def sides(n, lr, li, uc, us):
        lhs, cos_u, sin_u = [], [], []
        for ref in (lr, li):
            lhs += [ref[pl.ds((n // 4) * SUB * 8 + (2 * n + b) % 8, SUB, stride=8), :].astype(jnp.bfloat16) for b in range(2)]
        for b in range(2):
            at = pl.ds((n // 4) * half_u * 8 + (2 * n + b) % 8, half_u, stride=8)
            cos_u.append(uc[at, :].astype(jnp.bfloat16))
            sin_u.append(us[at, :].astype(jnp.bfloat16))
        neg_u = [-x for x in sin_u]
        rhs = [cos_u + neg_u, cos_u + sin_u, sin_u + cos_u, neg_u + cos_u]
        return jnp.concatenate(lhs, 1), [jnp.concatenate(r, 1) for r in rhs]

    def products(keep, send, n, *refs):
        made = [sides(4 * n + j, *refs) for j in range(4)]
        out = lax.dot_general(
            jnp.concatenate([m[0] for m in made], 0),
            jnp.concatenate(sum([m[1] for m in made], []), 0),
            (((1,), (1,)), ((), ())),
            preferred_element_type=jnp.float32,
        )
        group = max(1, 8 // Q)
        for j in range(4):
            mine = out[SUB * j : SUB * (j + 1), LANES * (j // 2) : LANES * (j // 2 + 1)]
            for g in range(4):
                x = mine[8 * g : 8 * g + 8]
                if j % 2:
                    x = jnp.where(low, pltpu.roll(x, LANES // 2, 1), pltpu.roll(x, 8 - Q2, 0))
                else:
                    x = jnp.where(low, x, pltpu.roll(pltpu.roll(x, 8 - Q2, 0), LANES // 2, 1))
                x = x.astype(jnp.bfloat16)
                for k in range(group):
                    d = g * group + k
                    place = bit_reverse(d // 2, T // 2)
                    ref = send if d % 2 else keep
                    ref[place, 4 * n + j] = x[k * Q : k * Q + Q2]

    for copy in numbers:
        copy.wait()
    sides_of = [tables[0:4], tables[4:8]]
    total = L // G

    def arrive(k):
        loads[2 * k].wait()
        loads[2 * k + 1].wait()
        vs[k * span : (k + 1) * span, :] = vis[k * span : (k + 1) * span, :].astype(jnp.float32)

    def make(i, side):
        at = pl.ds(pl.multiple_of(i * G * 4, 8), G * 4)
        for n in range(G // 4):
            powers(i * G, n, cs.at[at, :], vs.at[at, :], *sides_of[side])

    def use(i, side):
        at = pl.ds(i * G, G)
        for n in range(G // 4):
            products(keep.at[:, at], send.at[:, at], n, *sides_of[side])

    def step(j, carry):
        make(2 * j + 1, 1)
        use(2 * j, 0)
        make(2 * j + 2, 0)
        use(2 * j + 1, 1)
        return carry

    arrive(0)
    make(0, 0)
    for k in range(1, parts):
        arrive(k)
    lax.fori_loop(0, total // 2 - 1, step, 0)
    make(total - 1, 1)
    use(total - 2, 0)
    use(total - 1, 1)


def images(T, L, counts, offsets, coords, vis):
    Q2, G = SUB // T // 2, GROUP
    half = jax.ShapeDtypeStruct((T // 2, L, Q2, LANES), jnp.bfloat16)
    hbm, vmem = pl.BlockSpec(memory_space=pltpu.HBM), pl.BlockSpec(memory_space=pltpu.VMEM)
    table = lambda n: pltpu.VMEM((2 * G * n, LANES), jnp.float32)
    return pl.pallas_call(
        functools.partial(images_kernel, T, L, G),
        out_shape=(half, half),
        in_specs=[hbm] * 4,
        out_specs=(vmem, vmem),
        scratch_shapes=[pltpu.VMEM((4 * L, LANES), jnp.float32)] * 2
        + [
            pltpu.VMEM((4 * L, LANES), jnp.bfloat16),
            pltpu.SMEM((1, L), jnp.int32),
            pltpu.SMEM((2, L), jnp.int32),
            pltpu.SemaphoreType.DMA((6,)),
        ]
        + [table(SUB), table(SUB), table(SUB // 2), table(SUB // 2)] * 2,
        name="images",
        **PARAMS,
    )(*[pltpu.with_memory_space_constraint(x, pltpu.HBM) for x in (counts, offsets, coords, vis)])


def index_kernel(T, L, B, cap, capx, held, owners, stations, screens, first, second, hot, partial, rows):
    Q2 = SUB // T // 2
    F = Q2 * LANES
    a, base = lax.axis_index("tm"), lax.axis_index("base")
    mine = jnp.broadcast_to(owners[pl.ds(base, 1), :], (L, L))
    same = (mine == mine.T) & (iota((L, L), 0) < iota((L, L), 1))
    rank = jnp.sum(same.astype(jnp.float32), axis=0, keepdims=True).astype(jnp.int32)
    slots = mine[0:1] * capx + rank
    hot[...] = (iota((B * capx, L), 0) == slots).astype(jnp.float32).astype(jnp.bfloat16)
    for k, term in enumerate((first, second)):
        rows[k] = term[0].astype(jnp.float32).reshape(L * Q2, LANES)
    for q in range(Q2):
        parts = [rows[k, pl.ds(q, L, stride=Q2), :].astype(jnp.bfloat16) for k in range(2)]
        parts = [jnp.dot(hot[...], x, preferred_element_type=jnp.float32) for x in parts]
        partial[:, LANES * q : LANES * (q + 1)] = parts[0] + parts[1]

    lane = iota((1, F), 1)
    m = T * (((lane // (2 * SUB)) % 2) * Q2 + lane // LANES) + a
    pixel = m * SUB + column_of(lane % SUB)
    select = (iota((SUB * SUB, F), 0) == pixel).astype(jnp.float32).astype(jnp.bfloat16)
    x = jnp.concatenate([screens[:, 0, :].astype(jnp.float32), screens[:, 1, :].astype(jnp.float32)], 0)
    x = jnp.dot(x.astype(jnp.bfloat16), select, preferred_element_type=jnp.float32)
    mine_x = jnp.where((lane // SUB) % 2 == 0, x[:held], x[held:])
    mine_x = jnp.concatenate([mine_x, jnp.zeros((8 - held, F), jnp.float32)], 0)

    p, q = stations[0:1, :], stations[1:2, :]
    names = jnp.concatenate([jnp.zeros((4, L), jnp.int32), p // held, p % held, q // held, q % held], 0)
    names = names.astype(jnp.float32).astype(jnp.bfloat16)

    def one(o, carry):
        own = (iota((LANES, L), 0) + o * capx == slots).astype(jnp.float32).astype(jnp.bfloat16)
        listed = lax.dot_general(names, own, (((1,), (1,)), ((), ())), preferred_element_type=jnp.float32)
        listed = jnp.concatenate([listed] + [jnp.zeros((8, F - LANES), jnp.float32)], 1)
        at = pl.ds(pl.multiple_of(o * capx + cap, 8), 8)
        partial[at, :] = jnp.where(iota((8, F), 0) < 4, mine_x, listed)
        return carry

    lax.fori_loop(0, B, one, 0, unroll=min(B, 8))


def index_tables(T, L, B, cap, capx, held, owners, stations, screens, first, second):
    F = SUB // T // 2 * LANES
    vmem = pl.BlockSpec(memory_space=pltpu.VMEM)
    return pl.pallas_call(
        functools.partial(index_kernel, T, L, B, cap, capx, held),
        out_shape=(
            jax.ShapeDtypeStruct((B * capx, L), jnp.bfloat16),
            jax.ShapeDtypeStruct((B * capx, F), jnp.float32),
        ),
        in_specs=[vmem] * 5,
        out_specs=(vmem, vmem),
        scratch_shapes=[pltpu.VMEM((2, L * SUB // T // 2, LANES), jnp.float32)],
        name="index",
        cost_estimate=pl.CostEstimate(flops=10**7, bytes_accessed=10**6, transcendentals=0),
        **PARAMS,
    )(owners, stations, screens, first, second)


def send_kernel(T, L, B, cap, capx, *refs):
    terms, (hot, partial, out, rows, block, sems) = refs[:-6], refs[-6:]
    Q2 = SUB // T // 2
    total = terms[0][0].astype(jnp.float32)
    for t in terms[1:]:
        total = total + t[0].astype(jnp.float32)
    rows[...] = total.reshape(L * Q2, LANES)
    copies = []
    for q in range(Q2):
        at = slice(LANES * q, LANES * (q + 1))
        x = rows[pl.ds(q, L, stride=Q2), :].astype(jnp.bfloat16)
        moved = partial[:, at] + jnp.dot(hot[...], x, preferred_element_type=jnp.float32)
        block[:, :, at] = moved.astype(jnp.bfloat16).reshape(B, capx, LANES)
        copies.append(pltpu.make_async_copy(block.at[:, :, at], out.at[:, :, at], sems.at[q]))
        copies[-1].start()
    for copy in copies:
        copy.wait()


def send_blocks(T, L, B, cap, capx, terms, hot, partial):
    Q2 = SUB // T // 2
    F = Q2 * LANES
    vmem = pl.BlockSpec(memory_space=pltpu.VMEM)
    return pl.pallas_call(
        functools.partial(send_kernel, T, L, B, cap, capx),
        out_shape=jax.ShapeDtypeStruct((B, capx, F), jnp.bfloat16),
        in_specs=[vmem] * (len(terms) + 2),
        out_specs=pl.BlockSpec(memory_space=pltpu.HBM),
        scratch_shapes=[
            pltpu.VMEM((L * Q2, LANES), jnp.float32),
            pltpu.VMEM((B, capx, F), jnp.bfloat16),
            pltpu.SemaphoreType.DMA((Q2,)),
        ],
        name="send",
        **PARAMS,
    )(*terms, hot, partial)


def rows_kernel(T, S, row_off, rows):
    Q2 = SUB // T // 2
    K = 2 * Q2 * S
    chunk, half = TILE // T, TILE // 2
    a = lax.axis_index("tm")
    index = iota((1, K), 1) // S
    m = (T * ((index % 2) * Q2 + index // 2) + a).astype(jnp.float32) * (1.0 / SUB)
    er, ei = turn(iota((SUB, K), 0).astype(jnp.float32) * m)
    for d in range(T):
        for e in range(chunk // SUB):
            r = (a ^ d) * chunk + e * SUB + iota((SUB, K), 0) - row_off[...]
            mask = (r >= 0) & (r < SUB)
            at = bit_reverse(d // 2, T // 2) * chunk + e * SUB
            rows[d % 2, at : at + SUB, :] = jnp.where(mask, er, 0.0).astype(jnp.bfloat16)
            rows[d % 2, half + at : half + at + SUB, :] = jnp.where(mask, ei, 0.0).astype(jnp.bfloat16)


def row_tables(T, S, row_off):
    K = SUB // T * S
    vmem = pl.BlockSpec(memory_space=pltpu.VMEM)
    return pl.pallas_call(
        functools.partial(rows_kernel, T, S),
        out_shape=jax.ShapeDtypeStruct((2, TILE, K), jnp.bfloat16),
        in_specs=[vmem],
        out_specs=vmem,
        name="rows",
        cost_estimate=pl.CostEstimate(flops=10**7, bytes_accessed=10**6, transcendentals=0),
        **PARAMS,
    )(row_off)


def tile_part(T, rows, spread):
    both = jnp.dot(rows, spread, preferred_element_type=jnp.float32)
    u, v = both[: TILE // 2], both[TILE // 2 :]
    tile = jnp.concatenate([u[:, :TILE] + v[:, TILE:], u[:, TILE:] - v[:, :TILE]], 1)
    return tile.reshape(T // 2, TILE // T, 2 * TILE)


def place_kernel(T, B, cap, capx, held, blocks, col_off, rows, weights, spread, send, data, gains, hot):
    Q, Q2 = SUB // T, SUB // T // 2
    F = Q2 * LANES
    S = B * cap
    NX = B * 8
    a = lax.axis_index("tm")
    lane_f = iota((8, F), 1)
    part_f = (lane_f // SUB) % 2

    def gather(b, carry):
        data[pl.ds(b * cap, cap), :] = blocks[b, 0:cap, :].astype(jnp.float32)
        x = blocks[b, cap : cap + 8, :].astype(jnp.float32)
        at = pl.ds(pl.multiple_of(b * 8, 8), 8)
        gains[at, 0:F] = jnp.where(part_f == 0, x, pltpu.roll(x, SUB, 1))
        gains[at, F : 2 * F] = jnp.where(part_f == 1, x, pltpu.roll(x, F - SUB, 1))
        same = iota((cap, LANES), 0) == iota((cap, LANES), 1)
        for k in range(2):
            number = x[4 + 2 * k : 5 + 2 * k, 0:LANES] * 8.0 + x[5 + 2 * k : 6 + 2 * k, 0:LANES]
            number = jnp.sum(jnp.where(same, jnp.broadcast_to(number, (cap, LANES)), 0.0), axis=1, keepdims=True)
            hit = number.astype(jnp.int32) == iota((cap, NX), 1)
            hot[k, pl.ds(b * cap, cap), :] = hit.astype(jnp.float32)
        return carry

    lax.fori_loop(0, B, gather, 0, unroll=min(B, 8))

    hot_p, hot_q = hot[0].astype(jnp.bfloat16), hot[1].astype(jnp.bfloat16)
    lane = iota((1, LANES), 1)
    low, l = lane // (LANES // 2), column_of(lane % SUB)
    away = [(iota((S, LANES), 1) + LANES * v) - col_off[...] for v in range(2)]
    inside = [(w >= 0) & (w < SUB) for w in away]

    def taper(n):
        scaled = (n.astype(jnp.float32) + 0.5 - SUB / 2.0) / (SUB / 2.0)
        return 1.0 - scaled * scaled

    mixed = []
    for q in range(Q2):
        at = slice(LANES * q, LANES * (q + 1))
        at_i = slice(F + LANES * q, F + LANES * (q + 1))
        m = T * (low * Q2 + q) + a
        window = taper(m) * taper(l) * (1.0 / (SUB * 16.0))
        tables = [gains[:, at].astype(jnp.bfloat16), gains[:, at_i].astype(jnp.bfloat16)]
        pr, pi = [jnp.dot(hot_p, t, preferred_element_type=jnp.float32) for t in tables]
        qr, qi = [jnp.dot(hot_q, t, preferred_element_type=jnp.float32) for t in tables]
        d = data[:, at] * window
        x = jnp.concatenate([d * (pr * qr + pi * qi), d * (pr * qi - pi * qr)], 1).astype(jnp.bfloat16)
        mixed.append(x)

    for q in range(Q2):
        y = jnp.dot(mixed[q], weights[...], preferred_element_type=jnp.float32)
        for h in range(2):
            for c in range(2):
                v = y[:, (h * 2 + c) * LANES : (h * 2 + c + 1) * LANES]
                for half in range(2):
                    spread[pl.ds((q * 2 + h) * S, S), (c * 2 + half) * LANES : (c * 2 + half + 1) * LANES] = jnp.where(
                        inside[half], v, 0.0
                    ).astype(jnp.bfloat16)

    send[...] = tile_part(T, rows[1], spread[...]).astype(jnp.bfloat16)


def place_blocks(T, B, cap, capx, held, blocks, col_off, rows, weights):
    Q2 = SUB // T // 2
    F, S, K = Q2 * LANES, B * cap, 2 * Q2 * B * cap
    vmem = pl.BlockSpec(memory_space=pltpu.VMEM)
    return pl.pallas_call(
        functools.partial(place_kernel, T, B, cap, capx, held),
        out_shape=(
            jax.ShapeDtypeStruct((K, 2 * TILE), jnp.bfloat16),
            jax.ShapeDtypeStruct((T // 2, TILE // T, 2 * TILE), jnp.bfloat16),
        ),
        in_specs=[vmem] * 4,
        out_specs=(vmem, vmem),
        scratch_shapes=[
            pltpu.VMEM((S, F), jnp.float32),
            pltpu.VMEM((B * 8, 2 * F), jnp.float32),
            pltpu.VMEM((2, S, B * 8), jnp.float32),
        ],
        name="place",
        **PARAMS,
    )(blocks, col_off, rows, weights)


def keep_kernel(T, rows, spread, keep):
    keep[...] = tile_part(T, rows[0], spread[...])


def kept_rows(T, rows, spread):
    vmem = pl.BlockSpec(memory_space=pltpu.VMEM)
    return pl.pallas_call(
        functools.partial(keep_kernel, T),
        out_shape=jax.ShapeDtypeStruct((T // 2, TILE // T, 2 * TILE), jnp.float32),
        in_specs=[vmem] * 2,
        out_specs=vmem,
        name="keep",
        cost_estimate=pl.CostEstimate(flops=10**8, bytes_accessed=10**6, transcendentals=0),
        **PARAMS,
    )(rows, spread)


def transform_weights():
    lam = np.arange(SUB)
    l = np.where(lam < SUB // 2, lam + SUB // 2, SUB - 1 - lam)
    angle = 2.0 * math.pi * (l[:, None] * (np.arange(LANES)[None, :] % SUB) % SUB) / SUB
    cos, sin = np.cos(angle), np.sin(angle)
    out = np.zeros((2, 2, 2, SUB, 2, 2, LANES))
    for h in range(2):
        out[0, h, 0, :, h, 0], out[0, h, 0, :, h, 1] = cos, -sin
        out[0, h, 1, :, h, 0], out[0, h, 1, :, h, 1] = sin, cos
        out[1, h, 1, :, h, 0], out[1, h, 1, :, h, 1] = -cos, sin
        out[1, h, 0, :, h, 0], out[1, h, 0, :, h, 1] = sin, cos
    return jnp.asarray(out.reshape(2 * LANES, 4 * LANES), jnp.float32).astype(jnp.bfloat16)


def halve(T, keep, send, late=()):
    swap = lambda x, d: lax.ppermute(x, "tm", [(i, i ^ d) for i in range(T)])
    terms, d = [keep, swap(send, 1)], 2
    while d < T:
        half = T // d // 2
        moving = sum(t[half : 2 * half].astype(jnp.float32) for t in terms).astype(jnp.bfloat16)
        if late and d == 2:
            moving, *late = lax.optimization_barrier((moving, *late))
        terms.append(swap(moving, d))
        d *= 2
    return terms, late


def per_device(visibilities, coords, counts, stations, owners, offsets, screens):
    T, B = lax.axis_size("tm"), lax.axis_size("base")
    L, slots = visibilities.shape[1], visibilities.shape[3]
    base = lax.axis_index("base")
    Q2 = SUB // T // 2
    held = screens.shape[0]
    cap = -(-max(2, 3 * L // (2 * B)) // 8) * 8
    capx = cap + 8

    def flat(x):
        return x.reshape(L, 2, slots // LANES, LANES).transpose(0, 2, 1, 3).reshape(4 * L, LANES)

    keep, send = images(T, L, counts, offsets.T, flat(coords[0]), flat(visibilities[0]))
    terms, late = halve(T, keep, send, (owners, stations, screens))
    owner = late[0][:, 0].reshape(B, L)
    hot, partial = index_tables(T, L, B, cap, capx, held, owner, late[1].T, late[2], *terms[:2])
    outgoing = send_blocks(T, L, B, cap, capx, terms[2:], hot, partial)
    outgoing, owners, offsets = lax.optimization_barrier((outgoing, owners, offsets))

    to_me = owners[:, 0].reshape(B, L) == base
    order = jnp.arange(L, dtype=jnp.int32)
    earlier = order[:, None] < order[None, :]
    before = jnp.sum((to_me[:, :, None] & earlier[None]).astype(jnp.int32), axis=1)
    chosen = to_me[:, None, :] & (before[:, None, :] == jnp.arange(cap, dtype=jnp.int32)[None, :, None])
    offs = offsets.T.reshape(2, B, 1, L)
    slot_offs = jnp.sum(jnp.where(chosen[None], offs, 0), axis=3).reshape(2, B * cap)
    col_off = slot_offs[1][:, None]
    row_off = jnp.tile(slot_offs[0], 2 * Q2)[None, :]

    incoming = lax.all_to_all(outgoing, "base", split_axis=0, concat_axis=0, tiled=True)
    rows = row_tables(T, B * cap, row_off)
    spread, send = place_blocks(T, B, cap, capx, held, incoming, col_off, rows, transform_weights())
    terms, _ = halve(T, kept_rows(T, rows, spread), send)
    tile = sum(t[0].astype(jnp.float32) for t in terms)
    return tile.reshape(1, TILE // T, 2, TILE)


def solution(mesh):
    return jax.shard_map(
        per_device,
        mesh=mesh,
        in_specs=(
            P("tm", "base", None, None),
            P("tm", "base", None, None),
            P("tm", "base"),
            P("base", None),
            P(),
            P(),
            P("base", None, None),
        ),
        out_specs=P("base", "tm", None, None),
        check_vma=False,
    )
```
